32 devices in a mesh: shot: 16 (over z, y, x), det: 2 (over core).
Axes of the slice: x: 2, y: 2, z: 4, core: 2. Of those that a mesh axis runs over, the one named last changes fastest.
Arguments:
- events: int32 [16384, 2048], P('shot', 'det'), may hold values from 0 to 1, as said below
- pair_patches: int32 [2, 26, 2], P('det'), may hold values from 0 to 7, as said below
- pair_owners: int32 [2, 26, 2], P('det'), may hold values from 0 to 15, as said below
- triples: int32 [2, 256, 3], P('det'), may hold values from 0 to 1023, as said below
Outputs:
- intra_rates: float32 [16, 128, 128], P('det', 'shot')
- boundary_rates: float32 [2, 16, 6, 128, 128], P('det', 'shot')
- detector_load: float32 [16, 128], P(None, 'shot')
- triple_cumulant: float32 [2, 256], P('det')
The draws below stay inside these ranges and needn't reach their ends.
Inputs may be any that keep to these rules, and one draw needn't show every extreme that they name: events[s, i] is 1 where detector i fired in shot s, else 0. `pair_patches`: row d lists 26 blocks of panel d, each naming two different patches of the panel; no two blocks name the same two patches. `pair_owners`: of the 52 owner entries of one panel, no shot index is named more than 6 times, and in every panel some index is named exactly 6 times. `triples`: each triple holds three different detector indices of the panel in increasing order.
All inputs are finite; a program needn't handle non-finite values.
Results may differ from the reference program's by a relative error of at most 0.0003.
Values sent between devices are 32-bit elements; how exact they have to be, the bound alone decides.
A program may use at most 64 MiB of HBM per device.

```python
import jax
import jax.numpy as jnp
import numpy as np
from jax import lax

SHOT_DEV = 1024
PB = 128
PATCH_DEV = 8
PAIRS = 26
TRIPLES = 256
DET_DEV = 1024
PATCHES = 16
DETS = 2048
SHOTS = 16384
RECV = 6
N_SHOT = 16
N_DET = 2


def draw_events(key, part):
    key_list = jax.random.split(jax.random.fold_in(key, 11), 5)
    exponents = jax.random.randint(key_list[0], (DETS,), 3, 8)
    noisy_mask = jax.random.randint(key_list[1], (DETS,), 0, 32) == 0
    base_level = jnp.right_shift(jnp.int32(1 << 20), exponents)
    edge_level = jnp.right_shift(jnp.int32(1 << 20), jax.random.randint(key_list[2], (DETS,), 5, 10))
    hyper_level = jnp.right_shift(jnp.int32(1 << 20), jax.random.randint(key_list[3], (DETS,), 6, 10))
    span_steps = max(N_SHOT - 1, 1)

    def shot_block(block_index):
        block_keys = jax.random.split(jax.random.fold_in(key_list[4], block_index), 3)
        growth = span_steps + 2 * block_index
        noise_level = jnp.where(noisy_mask, 471859, base_level * growth // span_steps)
        single = jax.random.randint(block_keys[0], (SHOT_DEV, DETS), 0, 1 << 20) < noise_level[None, :]
        pairwise = jax.random.randint(block_keys[1], (SHOT_DEV, DETS), 0, 1 << 20) < (edge_level * growth // span_steps)[None, :]
        higher = jax.random.randint(block_keys[2], (SHOT_DEV, DETS), 0, 1 << 20) < (hyper_level * growth // span_steps)[None, :]
        flipped = single ^ pairwise ^ jnp.roll(pairwise, 1, axis=1) ^ higher ^ jnp.roll(higher, 1, axis=1) ^ jnp.roll(higher, 3, axis=1)
        return flipped.astype(jnp.int32)
    blocks = lax.map(shot_block, jnp.arange(N_SHOT, dtype=jnp.int32))
    return blocks.reshape(N_SHOT * SHOT_DEV, DETS)


def draw_pair_patches(key, part):
    first_np, second_np = np.triu_indices(PATCH_DEV, 1)
    pair_table = jnp.stack([jnp.asarray(first_np, jnp.int32), jnp.asarray(second_np, jnp.int32)], axis=1)

    def one_panel(panel_index):
        panel_key = jax.random.fold_in(jax.random.fold_in(key, 23), panel_index)
        first_key, second_key = jax.random.split(panel_key)
        picked = jax.random.permutation(first_key, pair_table.shape[0])[:PAIRS]
        chosen = pair_table[picked]
        reverse_bit = jax.random.randint(second_key, (PAIRS, 1), 0, 2)
        return jnp.where(reverse_bit == 1, chosen[:, ::-1], chosen).astype(jnp.int32)
    return lax.map(one_panel, jnp.arange(N_DET, dtype=jnp.int32))


def draw_pair_owners(key, part):

    def one_panel(panel_index):
        panel_key = jax.random.fold_in(jax.random.fold_in(key, 37), panel_index)
        first_key, second_key, third_key = jax.random.split(panel_key, 3)
        favored = jax.random.randint(first_key, (), 0, N_SHOT)
        spread = jax.random.permutation(second_key, (N_SHOT - 1) * RECV)[:2 * PAIRS - RECV] // RECV
        spread = spread + (spread >= favored).astype(jnp.int32)
        entries = jnp.concatenate([jnp.full((RECV,), favored, jnp.int32), spread.astype(jnp.int32)])
        entries = jax.random.permutation(third_key, entries)
        return entries.reshape(PAIRS, 2).astype(jnp.int32)
    return lax.map(one_panel, jnp.arange(N_DET, dtype=jnp.int32))


def draw_triples(key, part):
    first_key, second_key, third_key = jax.random.split(jax.random.fold_in(key, 53), 3)
    starts = jax.random.randint(first_key, (N_DET, TRIPLES), 0, PATCH_DEV * PB - 4)
    step_one = jax.random.randint(second_key, (N_DET, TRIPLES), 1, 3)
    step_two = jax.random.randint(third_key, (N_DET, TRIPLES), 1, 3)
    return jnp.stack([starts, starts + step_one, starts + step_one + step_two], axis=-1).astype(jnp.int32)


def setup_inputs(seed: int = 0) -> dict:
    keys = jax.random.split(jax.random.key(seed), 5)
    return {
        "events": draw_events(jax.random.fold_in(keys[4], 71), 0),
        "pair_patches": draw_pair_patches(jax.random.fold_in(keys[4], 71), 0),
        "pair_owners": draw_pair_owners(jax.random.fold_in(keys[4], 71), 0),
        "triples": draw_triples(jax.random.fold_in(keys[4], 71), 0),
    }


def fit_rates(coincide, row_count, col_count, shot_total):
    inverse = 1.0 / shot_total
    joint_rate = coincide * inverse
    row_rate = row_count[..., :, None] * inverse
    col_rate = col_count[..., None, :] * inverse
    denominator = jnp.maximum(1.0 - 2.0 * row_rate - 2.0 * col_rate + 4.0 * joint_rate, 0.25)
    excess = (joint_rate - row_rate * col_rate) / denominator
    return 100.0 * (0.5 - 0.5 * jnp.sqrt(jnp.maximum(1.0 - 4.0 * excess, 0.04)))

def route_table(owner_row, shot_count, recv_slots):
    owner_ids = jnp.arange(shot_count, dtype=jnp.int32)
    hit = owner_row[None, :] == owner_ids[:, None]
    rank = jnp.cumsum(hit.astype(jnp.int32), axis=1) - 1
    slot_ids = jnp.arange(recv_slots, dtype=jnp.int32)
    chosen = hit[:, None, :] & (rank[:, None, :] == slot_ids[None, :, None])
    entry_pair = jnp.arange(owner_row.shape[0], dtype=jnp.int32) // 2
    pair_slot = lax.optimization_barrier(jnp.sum(jnp.where(chosen, entry_pair[None, None, :], 0), axis=2)).astype(jnp.int32)
    valid = jnp.any(chosen, axis=2).astype(jnp.float32)
    return (pair_slot, valid)

def reference(events, pair_patches, pair_owners, triples):
    shot_total = float(SHOTS)
    inverse = 1.0 / shot_total
    counts = lax.optimization_barrier(jnp.sum(events, axis=0)).astype(jnp.float32)
    patch_counts = counts.reshape(PATCHES, PB)

    def patch_gram(patch_index):
        columns = lax.dynamic_slice_in_dim(events, (patch_index * PB).astype(jnp.int32), PB, 1).astype(jnp.float32)
        return jnp.dot(columns.T, columns, precision=lax.Precision.HIGHEST, preferred_element_type=jnp.float32)
    grams = lax.map(patch_gram, jnp.arange(PATCHES, dtype=jnp.int32))
    intra_rates = fit_rates(grams, patch_counts, patch_counts, shot_total)
    detector_load = lax.optimization_barrier(jnp.sum(intra_rates, axis=2))
    offsets = jnp.arange(N_DET, dtype=jnp.int32)[:, None, None] * PATCH_DEV
    pair_ends = (pair_patches + offsets).reshape(N_DET * PAIRS, 2).astype(jnp.int32)

    def pair_gram(ends):
        first_columns = lax.dynamic_slice_in_dim(events, (ends[0] * PB).astype(jnp.int32), PB, 1).astype(jnp.float32)
        second_columns = lax.dynamic_slice_in_dim(events, (ends[1] * PB).astype(jnp.int32), PB, 1).astype(jnp.float32)
        return jnp.dot(first_columns.T, second_columns, precision=lax.Precision.HIGHEST, preferred_element_type=jnp.float32)
    pair_grams = lax.map(pair_gram, pair_ends)
    pair_rates = fit_rates(pair_grams, patch_counts[pair_ends[:, 0]], patch_counts[pair_ends[:, 1]], shot_total)
    pair_slot, valid = jax.vmap(lambda owner_row: route_table(owner_row, N_SHOT, RECV))(pair_owners.reshape(N_DET, 2 * PAIRS))
    flat_index = (jnp.arange(N_DET, dtype=jnp.int32)[:, None, None] * PAIRS + pair_slot).reshape(-1)
    boundary_rates = jnp.take(pair_rates, flat_index, axis=0).reshape(N_DET, N_SHOT, RECV, PB, PB)
    boundary_rates = boundary_rates * valid[:, :, :, None, None]
    global_triples = (triples + jnp.arange(N_DET, dtype=jnp.int32)[:, None, None] * DET_DEV).astype(jnp.int32)

    def triple_sums(index_set):
        picked = jnp.take(events, index_set.reshape(-1), axis=1).astype(jnp.float32).reshape(SHOTS, TRIPLES, 3)
        first_bit = picked[:, :, 0]
        second_bit = picked[:, :, 1]
        third_bit = picked[:, :, 2]
        return jnp.stack([lax.optimization_barrier(jnp.sum(first_bit * second_bit, axis=0)), lax.optimization_barrier(jnp.sum(first_bit * third_bit, axis=0)), lax.optimization_barrier(jnp.sum(second_bit * third_bit, axis=0)), lax.optimization_barrier(jnp.sum(first_bit * second_bit * third_bit, axis=0))])
    moments = lax.map(triple_sums, global_triples) * inverse
    means = counts[global_triples] * inverse
    mean_first = means[:, :, 0]
    mean_second = means[:, :, 1]
    mean_third = means[:, :, 2]
    kappa = moments[:, 3] - moments[:, 0] * mean_third - moments[:, 1] * mean_second - moments[:, 2] * mean_first + 2.0 * mean_first * mean_second * mean_third
    triple_cumulant = 1000.0 * kappa
    return (intra_rates, boundary_rates, detector_load, triple_cumulant)
```

```python
import functools

import jax
import jax.numpy as jnp
from jax import lax
from jax.experimental import pallas as pl
from jax.experimental.pallas import tpu as pltpu
from jax.sharding import PartitionSpec as P

PB = 128


def fit_rates(coincide, row_count, col_count, shot_total):
    inverse = 1.0 / shot_total
    joint_rate = coincide * inverse
    row_rate = row_count[..., :, None] * inverse
    col_rate = col_count[..., None, :] * inverse
    denominator = jnp.maximum(1.0 - 2.0 * row_rate - 2.0 * col_rate + 4.0 * joint_rate, 0.25)
    excess = (joint_rate - row_rate * col_rate) / denominator
    return 100.0 * (0.5 - 0.5 * jnp.sqrt(jnp.maximum(1.0 - 4.0 * excess, 0.04)))


def route_table(owner_row, shot_count, recv_slots):
    owner_ids = jnp.arange(shot_count, dtype=jnp.int32)
    hit = owner_row[None, :] == owner_ids[:, None]
    entry_ids = jnp.arange(owner_row.shape[0], dtype=jnp.int32)
    upto = entry_ids[:, None] >= entry_ids[None, :]
    rank = jnp.sum(jnp.where(hit[:, None, :] & upto[None, :, :], 1, 0), axis=2) - 1
    slot_ids = jnp.arange(recv_slots, dtype=jnp.int32)
    chosen = hit[:, None, :] & (rank[:, None, :] == slot_ids[None, :, None])
    entry_pair = jnp.arange(owner_row.shape[0], dtype=jnp.int32) // 2
    pair_slot = jnp.sum(jnp.where(chosen, entry_pair[None, None, :], 0), axis=2)
    valid = jnp.any(chosen, axis=2).astype(jnp.float32)
    return (pair_slot, valid)


def plan_streams(shot_count, block_count):
    bits = shot_count.bit_length() - 1
    ids = list(range(bits))
    if bits < 3:
        return [(tuple(ids), 0, block_count)]
    rest = ids[2:]
    along_x, along_y, along_z = (0, 1, *rest), (1, 0, *rest), (*rest, 0, 1)
    deep = max(1, block_count * 2 // 9)
    left = block_count - deep
    sizes = [left // 4, (left + 1) // 4, deep, (left + 2) // 4, (left + 3) // 4]
    orders = [along_x, along_y, along_z, along_x, along_y]
    streams = []
    start = 0
    for order, size in zip(orders, sizes):
        streams.append((order, start, size))
        start += size
    return streams


def finish_kernel(intra_in, boundary_in, load_in, kappa_in, intra_out, boundary_out, load_out, kappa_out,
                  intra_buf, boundary_buf, load_buf, kappa_buf, in_sem, out_sem):
    halves = boundary_in.shape[0] // 2
    moves = [(boundary_in.at[pl.ds(0, halves)], boundary_buf.at[pl.ds(0, halves)], boundary_out.at[pl.ds(0, halves)]),
             (boundary_in.at[pl.ds(halves, halves)], boundary_buf.at[pl.ds(halves, halves)],
              boundary_out.at[pl.ds(halves, halves)]),
             (intra_in, intra_buf, intra_out)]
    arrive = [pltpu.make_async_copy(source, held, in_sem.at[i]) for i, (source, held, _) in enumerate(moves)]
    arrive += [pltpu.make_async_copy(load_in, load_buf, in_sem.at[3]),
               pltpu.make_async_copy(kappa_in, kappa_buf, in_sem.at[4])]
    leave = [pltpu.make_async_copy(held, target, out_sem.at[i]) for i, (_, held, target) in enumerate(moves)]
    for copy in arrive:
        copy.start()
    for copy, onward in zip(arrive, leave):
        copy.wait()
        onward.start()
    arrive[3].wait()
    arrive[4].wait()
    total = load_buf[0]
    for d in range(1, load_buf.shape[0]):
        total = total + load_buf[d]
    load_out[...] = total[:, 0:load_out.shape[1]]
    kappa_out[...] = kappa_buf[...]
    for copy in leave:
        copy.wait()


def fused_kernel(plan, events_ref, ends_ref, owner_ref, triple_ref, intra_ref, boundary_ref, load_ref,
                 kappa_ref, *scratch):
    (streams, shot_count, det_count, patch_dev, pair_count, triple_count, recv_slots, load_chunks) = plan
    bits = shot_count.bit_length() - 1
    scratch = list(scratch)
    raw, turned, aux, aux_in, share, row_buf, col_buf, fitted, outgoing, load_mine, route = scratch[:11]
    in_sem, send_sem, recv_sem, aux_send, aux_recv, out_send, out_recv, own_sem, load_send, load_recv, relay = scratch[11:22]
    held = scratch[22:22 + len(streams)]
    landed = [scratch[22 + len(streams) + s * bits:22 + len(streams) + (s + 1) * bits] for s in range(len(streams))]
    shot_dev, det_dev = raw.shape
    block_rows = PB // shot_count
    me = lax.axis_index("shot")
    my_det = lax.axis_index("det")
    shot_total = float(shot_dev * shot_count)
    inverse = 1.0 / shot_total
    bit = [(me // (1 << b)) % 2 for b in range(bits)]
    partner = [me + (1 - 2 * bit[b]) * (1 << b) for b in range(bits)]

    chunk = shot_dev // load_chunks
    copies = []
    for c in range(load_chunks):
        copy = pltpu.make_async_copy(
            events_ref.at[pl.ds(c * chunk, chunk), :], raw.at[pl.ds(c * chunk, chunk), :], in_sem.at[c])
        copy.start()
        copies.append(copy)
    barrier = pltpu.get_barrier_semaphore()
    line = bits > 3
    for b in range(min(bits, 2) if line else bits):
        pl.semaphore_signal(barrier, inc=1, device_id={"shot": partner[b]}, device_id_type=pl.DeviceIdType.MESH)
    has_up, has_down = me + 4 < shot_count, me >= 4

    def signal_line(sem):
        @pl.when(has_up)
        def _():
            pl.semaphore_signal(sem, inc=1, device_id={"shot": me + 4}, device_id_type=pl.DeviceIdType.MESH)

        @pl.when(has_down)
        def _():
            pl.semaphore_signal(sem, inc=1, device_id={"shot": me - 4}, device_id_type=pl.DeviceIdType.MESH)

    if line:
        signal_line(barrier)
    line_count = has_up.astype(jnp.int32) + has_down.astype(jnp.int32)
    greeted = 2 + line_count if line else bits
    for d in range(1, det_count):
        pl.semaphore_signal(barrier, inc=1, device_id={"det": (my_det + d) % det_count},
                            device_id_type=pl.DeviceIdType.MESH)
    for c in range(load_chunks):
        copies[c].wait()
        piece = raw[pl.ds(c * chunk, chunk), :].astype(jnp.float32).astype(jnp.bfloat16)
        turned[:, :, pl.ds(c * chunk, chunk)] = piece.T.reshape(patch_dev, PB, chunk)

    nt = (((1,), (1,)), ((), ()))

    def stream_copy(s, t):
        order, _, size = streams[s]
        base = 0
        for i in range(t):
            base = base + bit[order[i]] * (1 << (bits - 1 - i))
        length = 1 << (bits - 1 - t)
        away = base + (1 - bit[order[t]]) * length
        return pltpu.make_async_remote_copy(
            src_ref=held[s].at[pl.ds(away, length)], dst_ref=landed[s][t],
            send_sem=send_sem.at[s, t], recv_sem=recv_sem.at[s, t],
            device_id={"shot": partner[order[t]]}, device_id_type=pl.DeviceIdType.MESH)

    def put_block(s, first, second, position):
        order = streams[s][0]
        left = turned[first]
        right = turned[second]
        gram = lax.dot_general(left, right, nt, preferred_element_type=jnp.float32)
        for g in range(shot_count):
            index = sum(((g >> order[i]) & 1) << (bits - 1 - i) for i in range(bits))
            held[s][index, position] = gram[g * block_rows:(g + 1) * block_rows]

    for s, (order, start, size) in enumerate(streams):
        split = min(max(patch_dev - start, 0), size)
        if split:
            @pl.loop(0, split, unroll=True)
            def _(k):
                put_block(s, start + k, start + k, k)
        if size > split:
            @pl.loop(split, size, unroll=True)
            def _(k):
                pair = start + k - patch_dev
                put_block(s, ends_ref[0, pair], ends_ref[1, pair], k)
        if s == 0:
            pl.semaphore_wait(barrier, greeted + det_count - 1)
            if line:
                signal_line(relay)
        stream_copy(s, 0).start()

    ones = jnp.ones((8, shot_dev), jnp.bfloat16)
    for p in range(patch_dev):
        total = lax.dot_general(ones, turned[p], nt, preferred_element_type=jnp.float32)
        aux[0, pl.ds(p, 1), :] = total[0:1]
    lane = lax.broadcasted_iota(jnp.int32, (PB, 128), 1)
    for c in range(triple_count // 128):
        column = lax.broadcasted_iota(jnp.int32, (128, det_dev), 1)
        bit_rows = []
        for m in range(3):
            named = jnp.broadcast_to(triple_ref[m, :, pl.ds(c * 128, 128)], (128, 128)).T[:, 0:1]
            bit_rows.append(
                jnp.dot((named == column).astype(jnp.float32).astype(jnp.bfloat16),
                        turned[...].reshape(det_dev, shot_dev), preferred_element_type=jnp.float32))
        one, two, three = bit_rows
        both = one * two
        terms = [one, two, three, both, one * three, two * three, both * three]
        packed = jnp.zeros((128, 128), jnp.float32)
        for q, term in enumerate(terms):
            packed = jnp.where(lane == q, jnp.sum(term, axis=1, keepdims=True), packed)
        aux[0, pl.ds(patch_dev + 8 * c, 8), :] = packed.T[0:8]

    slots = shot_count * recv_slots
    slot_id = lax.broadcasted_iota(jnp.int32, (slots, 1), 0)
    slot_owner = jnp.zeros((slots, 1), jnp.int32)
    for owner in range(1, shot_count):
        slot_owner = slot_owner + (slot_id >= owner * recv_slots).astype(jnp.int32)
    slot_rank = (slot_id - slot_owner * recv_slots).astype(jnp.float32)
    hit_first = (owner_ref[0:1, :] == slot_owner).astype(jnp.float32)
    hit_second = (owner_ref[1:2, :] == slot_owner).astype(jnp.float32)
    earlier = (lax.broadcasted_iota(jnp.int32, (pair_count, pair_count), 0)
               < lax.broadcasted_iota(jnp.int32, (pair_count, pair_count), 1)).astype(jnp.float32)
    rank_first = jnp.dot((hit_first + hit_second).astype(jnp.bfloat16), earlier.astype(jnp.bfloat16),
                         preferred_element_type=jnp.float32)
    rank_second = rank_first + hit_first
    route[...] = (jnp.where(rank_first == slot_rank, hit_first, 0.0)
                  + jnp.where(rank_second == slot_rank, hit_second, 0.0))

    def aux_copy(t):
        return pltpu.make_async_remote_copy(
            src_ref=aux.at[t], dst_ref=aux_in.at[t], send_sem=aux_send.at[t], recv_sem=aux_recv.at[t],
            device_id={"shot": partner[t]}, device_id_type=pl.DeviceIdType.MESH)

    if line:
        pl.semaphore_wait(relay, line_count)
    aux_copy(0).start()
    visit = list(range(len(streams)))
    for t in range(bits):
        for s in visit:
            order, start, size = streams[s]
            stream_copy(s, t).wait_recv()
            base = 0
            for i in range(t):
                base = base + bit[order[i]] * (1 << (bits - 1 - i))
            length = 1 << (bits - 1 - t)
            base = base + bit[order[t]] * length
            if t < bits - 1:
                half = length // 2
                away = (1 - bit[order[t + 1]]) * half
                keep = bit[order[t + 1]] * half

                @pl.loop(0, half)
                def _(i):
                    held[s][base + away + i] = held[s][base + away + i] + landed[s][t][away + i]
                stream_copy(s, t + 1).start()

                @pl.loop(0, half)
                def _(i):
                    held[s][base + keep + i] = held[s][base + keep + i] + landed[s][t][keep + i]
            else:
                share[pl.ds(start, size)] = held[s][base] + landed[s][t][0]
        aux_copy(t).wait_recv()
        aux[t + 1] = aux[t] + aux_in[t]
        if t < bits - 1:
            aux_copy(t + 1).start()

    row = lax.broadcasted_iota(jnp.int32, (block_rows, PB), 0)
    col = lax.broadcasted_iota(jnp.int32, (block_rows, PB), 1)
    on_diagonal = col == row + me * block_rows

    def rates(coincide, row_rate, col_rate):
        joint_rate = coincide * inverse
        denominator = jnp.maximum(1.0 - 2.0 * row_rate - 2.0 * col_rate + 4.0 * joint_rate, 0.25)
        excess = (joint_rate - row_rate * col_rate) / denominator
        return 100.0 * (0.5 - 0.5 * jnp.sqrt(jnp.maximum(1.0 - 4.0 * excess, 0.04)))

    loads = jnp.zeros((block_rows, PB), jnp.float32)
    for p in range(patch_dev):
        block = share[p]
        row_rate = jnp.broadcast_to(
            jnp.sum(jnp.where(on_diagonal, block, 0.0), axis=1, keepdims=True), block.shape) * inverse
        col_rate = jnp.broadcast_to(aux[bits, pl.ds(p, 1), :], block.shape) * inverse
        row_buf[p] = row_rate
        col_buf[p] = col_rate
        fit = rates(block, row_rate, col_rate)
        intra_ref[p] = fit
        loads = jnp.where(col == my_det * patch_dev + p, jnp.sum(fit, axis=1, keepdims=True), loads)
    load_mine[...] = loads

    @pl.loop(0, pair_count)
    def _(k):
        fitted[k] = rates(share[patch_dev + k], row_buf[ends_ref[0, k]], col_buf[ends_ref[1, k]])

    chosen = jnp.dot(route[...], fitted[...].reshape(pair_count, block_rows * PB),
                     precision=lax.Precision.HIGHEST, preferred_element_type=jnp.float32)
    outgoing[...] = chosen.reshape(shot_count, recv_slots, block_rows, PB)

    def out_copy(d):
        other = (me + d) % shot_count
        return pltpu.make_async_remote_copy(
            src_ref=outgoing.at[other],
            dst_ref=boundary_ref.at[:, pl.ds(pl.multiple_of(me * block_rows, block_rows), block_rows), :],
            send_sem=out_send.at[d], recv_sem=out_recv.at[d],
            device_id={"shot": other}, device_id_type=pl.DeviceIdType.MESH)

    def load_copy(d):
        return pltpu.make_async_remote_copy(
            src_ref=load_mine, dst_ref=load_ref.at[my_det], send_sem=load_send.at[d], recv_sem=load_recv.at[d],
            device_id={"det": (my_det + d) % det_count}, device_id_type=pl.DeviceIdType.MESH)

    for d in range(1, shot_count):
        out_copy(d).start()
    for d in range(1, det_count):
        load_copy(d).start()
    own = pltpu.make_async_copy(
        outgoing.at[me], boundary_ref.at[:, pl.ds(pl.multiple_of(me * block_rows, block_rows), block_rows), :],
        own_sem)
    own.start()
    load_ref[my_det] = loads

    for c in range(triple_count // 128):
        sums = aux[bits, pl.ds(patch_dev + 8 * c, 8), :] * inverse
        first, second, third = sums[0:1], sums[1:2], sums[2:3]
        kappa = (sums[6:7] - sums[3:4] * third - sums[4:5] * second - sums[5:6] * first
                 + 2.0 * first * second * third)
        kappa_ref[:, pl.ds(c * 128, 128)] = 1000.0 * kappa

    own.wait()
    for d in range(1, det_count):
        load_copy(d).wait()
    for d in range(1, shot_count):
        out_copy(d).wait()
    for t in range(bits):
        aux_copy(t).wait_send()
        for s in range(len(streams)):
            stream_copy(s, t).wait_send()


def local_fused(events, pair_patches, pair_owners, triples, det_count):
    shot_dev, det_dev = events.shape
    shot_count = lax.axis_size("shot")
    bits = shot_count.bit_length() - 1
    patch_dev = det_dev // PB
    block_rows = PB // shot_count
    pair_count = pair_patches.shape[1]
    triple_count = triples.shape[1]
    recv_slots = max(2, 4 * pair_count // shot_count)
    block_count = patch_dev + pair_count
    streams = plan_streams(shot_count, block_count)
    load_chunks = 4
    smem = pl.BlockSpec(memory_space=pltpu.SMEM)
    vmem = pl.BlockSpec(memory_space=pltpu.VMEM)
    plan = (streams, shot_count, det_count, patch_dev, pair_count, triple_count, recv_slots, load_chunks)
    aux_rows = patch_dev + 8 * (triple_count // 128)
    f32 = jnp.float32
    dma = pltpu.SemaphoreType.DMA
    scratch = [
        pltpu.VMEM((shot_dev, det_dev), jnp.int32),
        pltpu.VMEM((patch_dev, PB, shot_dev), jnp.bfloat16),
        pltpu.VMEM((bits + 1, aux_rows, 128), f32),
        pltpu.VMEM((bits, aux_rows, 128), f32),
        pltpu.VMEM((block_count, block_rows, PB), f32),
        pltpu.VMEM((patch_dev, block_rows, PB), f32),
        pltpu.VMEM((patch_dev, block_rows, PB), f32),
        pltpu.VMEM((pair_count, block_rows, PB), f32),
        pltpu.VMEM((shot_count, recv_slots, block_rows, PB), f32),
        pltpu.VMEM((block_rows, PB), f32),
        pltpu.VMEM((shot_count * recv_slots, pair_count), f32),
        dma((load_chunks,)), dma((len(streams), bits)), dma((len(streams), bits)), dma((bits,)), dma((bits,)),
        dma((shot_count,)), dma((shot_count,)), dma, dma((det_count,)), dma((det_count,)),
        pltpu.SemaphoreType.REGULAR,
    ]
    scratch += [pltpu.VMEM((shot_count, size, block_rows, PB), f32) for _, _, size in streams]
    for _, _, size in streams:
        scratch += [pltpu.VMEM((1 << (bits - 1 - t), size, block_rows, PB), f32) for t in range(bits)]
    intra, boundary, load, kappa = pl.pallas_call(
        functools.partial(fused_kernel, plan),
        out_shape=(
            jax.ShapeDtypeStruct((patch_dev, block_rows, PB), f32),
            jax.ShapeDtypeStruct((recv_slots, PB, PB), f32),
            jax.ShapeDtypeStruct((det_count, block_rows, PB), f32),
            jax.ShapeDtypeStruct((1, triple_count), f32),
        ),
        in_specs=[pl.BlockSpec(memory_space=pltpu.HBM), smem, vmem, vmem],
        out_specs=(vmem, vmem, vmem, vmem),
        scratch_shapes=scratch,
        compiler_params=pltpu.CompilerParams(
            collective_id=0, has_side_effects=True, vmem_limit_bytes=58 * 1024 * 1024),
    )(events, jnp.swapaxes(pair_patches[0], 0, 1), jnp.swapaxes(pair_owners[0], 0, 1),
      jnp.transpose(triples, (2, 0, 1)))
    hbm = pl.BlockSpec(memory_space=pltpu.HBM)
    intra, boundary, load, kappa = pl.pallas_call(
        finish_kernel,
        out_shape=(
            jax.ShapeDtypeStruct((patch_dev, block_rows, PB), f32),
            jax.ShapeDtypeStruct((recv_slots, PB, PB), f32),
            jax.ShapeDtypeStruct((block_rows, det_count * patch_dev), f32),
            jax.ShapeDtypeStruct((1, triple_count), f32),
        ),
        in_specs=[hbm, hbm, hbm, hbm],
        out_specs=(hbm, hbm, vmem, vmem),
        scratch_shapes=[
            pltpu.VMEM((patch_dev, block_rows, PB), f32),
            pltpu.VMEM((recv_slots, PB, PB), f32),
            pltpu.VMEM((det_count, block_rows, PB), f32),
            pltpu.VMEM((1, triple_count), f32),
            dma((5,)), dma((3,)),
        ],
        compiler_params=pltpu.CompilerParams(vmem_limit_bytes=61 * 1024 * 1024),
    )(intra, boundary, load, kappa)
    return (intra, boundary[None, None], jnp.swapaxes(load, 0, 1), kappa)


def local(events, pair_patches, pair_owners, triples):
    shot_dev, det_dev = events.shape
    shot_count = lax.axis_size("shot")
    shot_index = lax.axis_index("shot")
    shot_total = float(shot_dev * shot_count)
    inverse = 1.0 / shot_total
    patch_dev = det_dev // PB
    rows_own = PB // shot_count
    pair_count = pair_patches.shape[1]
    triple_count = triples.shape[1]
    recv_slots = max(2, 4 * pair_count // shot_count)
    bit_matrix = events.astype(jnp.bfloat16)
    patches = bit_matrix.reshape(shot_dev, patch_dev, PB)
    local_counts = jnp.sum(events, axis=0).astype(jnp.float32)
    triple_index = triples[0]
    picked = (
        jnp.take(events, triple_index.reshape(-1), axis=1)
        .astype(jnp.float32)
        .reshape(shot_dev, triple_count, 3)
    )
    first_bit = picked[:, :, 0]
    second_bit = picked[:, :, 1]
    third_bit = picked[:, :, 2]
    triple_terms = jnp.stack(
        [
            jnp.sum(first_bit * second_bit, axis=0),
            jnp.sum(first_bit * third_bit, axis=0),
            jnp.sum(second_bit * third_bit, axis=0),
            jnp.sum(first_bit * second_bit * third_bit, axis=0),
        ]
    )
    intra = jnp.einsum("sai,saj->aij", patches, patches, preferred_element_type=jnp.float32)
    pair_ends = pair_patches[0]

    def pair_gram(ends):
        first = lax.dynamic_slice_in_dim(bit_matrix, ends[0] * PB, PB, 1)
        second = lax.dynamic_slice_in_dim(bit_matrix, ends[1] * PB, PB, 1)
        return lax.dot_general(first, second, (((0,), (0,)), ((), ())), preferred_element_type=jnp.float32)

    cross = lax.map(pair_gram, pair_ends)
    joined = lax.psum_scatter(
        jnp.concatenate([intra, cross], axis=0), "shot", scatter_dimension=1, tiled=True
    )
    intra_share = joined[:patch_dev]
    pair_share = joined[patch_dev:]
    counts, triple_total = lax.psum((local_counts, triple_terms), "shot")
    patch_counts = counts.reshape(patch_dev, PB)
    row_counts = lax.dynamic_slice_in_dim(patch_counts, shot_index * rows_own, rows_own, 1)
    intra_rates = fit_rates(intra_share, row_counts, patch_counts, shot_total)
    load_share = jnp.sum(intra_rates, axis=2)
    detector_load = lax.all_gather(load_share, "det", axis=0, tiled=True)
    pair_slot, valid = route_table(pair_owners[0].reshape(-1), shot_count, recv_slots)
    mine = lax.dynamic_index_in_dim(pair_slot, shot_index, 0, keepdims=False)
    valid_mine = lax.dynamic_index_in_dim(valid, shot_index, 0, keepdims=False)
    fitted = fit_rates(
        pair_share,
        jnp.take(row_counts, pair_ends[:, 0], axis=0),
        jnp.take(patch_counts, pair_ends[:, 1], axis=0),
        shot_total,
    )
    every_block = lax.all_gather(fitted, "shot", axis=1, tiled=True)
    boundary = lax.map(lambda k: lax.dynamic_index_in_dim(every_block, k, 0, keepdims=False), mine)
    boundary = boundary * valid_mine[:, None, None]
    moments = triple_total * inverse
    means = jnp.take(counts, triple_index.reshape(-1), axis=0).reshape(triple_count, 3) * inverse
    mean_first = means[:, 0]
    mean_second = means[:, 1]
    mean_third = means[:, 2]
    kappa = (
        moments[3]
        - moments[0] * mean_third
        - moments[1] * mean_second
        - moments[2] * mean_first
        + 2.0 * mean_first * mean_second * mean_third
    )
    triple_cumulant = 1000.0 * kappa
    return (intra_rates, boundary[None, None], detector_load, triple_cumulant[None])


def solution(mesh):
    placed = (P("shot", "det"), P("det", None, None), P("det", None, None), P("det", None, None))
    shot_count = mesh.shape["shot"]
    det_count = mesh.shape["det"]
    power_of_two = shot_count & (shot_count - 1) == 0 and shot_count > 1
    whole_tiles = PB % shot_count == 0 and (PB // shot_count) % 8 == 0

    def body(events, pair_patches, pair_owners, triples):
        if power_of_two and whole_tiles and triples.shape[1] % 128 == 0:
            return local_fused(events, pair_patches, pair_owners, triples, det_count)
        return local(events, pair_patches, pair_owners, triples)

    return jax.shard_map(
        body,
        mesh=mesh,
        in_specs=placed,
        out_specs=(
            P("det", "shot", None),
            P("det", "shot", None, None, None),
            P(None, "shot"),
            P("det", None),
        ),
        check_vma=False,
    )
```

```python
import functools

import jax
import jax.numpy as jnp
from jax import lax
from jax.experimental import pallas as pl
from jax.experimental.pallas import tpu as pltpu
from jax.sharding import PartitionSpec as P

PB = 128


def fit_rates(coincide, row_count, col_count, shot_total):
    inverse = 1.0 / shot_total
    joint_rate = coincide * inverse
    row_rate = row_count[..., :, None] * inverse
    col_rate = col_count[..., None, :] * inverse
    denominator = jnp.maximum(1.0 - 2.0 * row_rate - 2.0 * col_rate + 4.0 * joint_rate, 0.25)
    excess = (joint_rate - row_rate * col_rate) / denominator
    return 100.0 * (0.5 - 0.5 * jnp.sqrt(jnp.maximum(1.0 - 4.0 * excess, 0.04)))


def route_table(owner_row, shot_count, recv_slots):
    owner_ids = jnp.arange(shot_count, dtype=jnp.int32)
    hit = owner_row[None, :] == owner_ids[:, None]
    entry_ids = jnp.arange(owner_row.shape[0], dtype=jnp.int32)
    upto = entry_ids[:, None] >= entry_ids[None, :]
    rank = jnp.sum(jnp.where(hit[:, None, :] & upto[None, :, :], 1, 0), axis=2) - 1
    slot_ids = jnp.arange(recv_slots, dtype=jnp.int32)
    chosen = hit[:, None, :] & (rank[:, None, :] == slot_ids[None, :, None])
    entry_pair = jnp.arange(owner_row.shape[0], dtype=jnp.int32) // 2
    pair_slot = jnp.sum(jnp.where(chosen, entry_pair[None, None, :], 0), axis=2)
    valid = jnp.any(chosen, axis=2).astype(jnp.float32)
    return (pair_slot, valid)


def plan_streams(bits, patch_dev, pair_count):
    x, y, low, high = range(bits)
    first = pair_count // 2
    a = (0, first)
    b = (first, pair_count - first)
    deep = patch_dev // 2
    side = (patch_dev - deep) // 2
    return [
        ("pair", 0, (x, y, low), *a),
        ("pair", 0, (y, x, low), *b),
        ("pair", 1, (x, y, low), *a),
        ("pair", 1, (y, x, low), *b),
        ("intra", 0, (low, high, x, y), 0, deep),
        ("intra", 0, (x, y, low, high), deep, side),
        ("intra", 0, (y, x, low, high), deep + side, patch_dev - deep - side),
    ]


PAIR_A0, PAIR_B0, PAIR_A1, PAIR_B1, DEEP, SIDE_X, SIDE_Y = range(7)
ORDER = [
    (PAIR_A0, 0), (PAIR_B0, 0), "first", (DEEP, 0), (SIDE_X, 0), (SIDE_Y, 0), ("aux", 0),
    (PAIR_A0, 1), (PAIR_B0, 1), ("aux", 1), (DEEP, 1), (SIDE_X, 1), (SIDE_Y, 1),
    (PAIR_A0, 2), (PAIR_B0, 2), ("aux", 2), (DEEP, 2),
    (PAIR_A1, 0), (PAIR_B1, 0), ("aux", 3), "means",
    (PAIR_A0, 3), (PAIR_B0, 3), ("route", 0),
    (PAIR_A1, 1), (PAIR_B1, 1), (SIDE_X, 2), (SIDE_Y, 2),
    (PAIR_A1, 2), (PAIR_B1, 2), (DEEP, 3), (SIDE_X, 3), (SIDE_Y, 3), "intra",
    (PAIR_A1, 3), (PAIR_B1, 3), ("route", 1),
]


def finish_kernel(intra_in, boundary_in, load_in, kappa_in, intra_out, boundary_out, load_out, kappa_out,
                  intra_buf, boundary_buf, load_buf, kappa_buf, in_sem, out_sem):
    halves = boundary_in.shape[0] // 2
    moves = [(boundary_in.at[pl.ds(0, halves)], boundary_buf.at[pl.ds(0, halves)], boundary_out.at[pl.ds(0, halves)]),
             (boundary_in.at[pl.ds(halves, halves)], boundary_buf.at[pl.ds(halves, halves)],
              boundary_out.at[pl.ds(halves, halves)]),
             (intra_in, intra_buf, intra_out)]
    arrive = [pltpu.make_async_copy(source, held, in_sem.at[i]) for i, (source, held, _) in enumerate(moves)]
    arrive += [pltpu.make_async_copy(load_in, load_buf, in_sem.at[3]),
               pltpu.make_async_copy(kappa_in, kappa_buf, in_sem.at[4])]
    leave = [pltpu.make_async_copy(held, target, out_sem.at[i]) for i, (_, held, target) in enumerate(moves)]
    for copy in arrive:
        copy.start()
    for copy, onward in zip(arrive, leave):
        copy.wait()
        onward.start()
    arrive[3].wait()
    arrive[4].wait()
    total = load_buf[0]
    for d in range(1, load_buf.shape[0]):
        total = total + load_buf[d]
    load_out[...] = total[:, 0:load_out.shape[1]]
    kappa_out[...] = kappa_buf[...]
    for copy in leave:
        copy.wait()


def fused_kernel(plan, events_ref, ends_ref, owner_ref, triple_ref, intra_ref, boundary_ref, load_ref,
                 kappa_ref, *scratch):
    (streams, shot_count, det_count, patch_dev, pair_count, triple_count, recv_slots, load_chunks, tiles) = plan
    bits = shot_count.bit_length() - 1
    count = len(streams)
    raw, turned, aux, aux_in, intra_sum, pair_sum, turned_counts, row_buf, col_buf, fitted, outgoing, load_mine = scratch[:12]
    slot_vector, slot_table = scratch[12:14]
    (in_sem, send_sem, recv_sem, aux_send, aux_recv, out_send, out_recv, load_send, load_recv, relay,
     table_sem) = scratch[14:25]
    held = scratch[25:25 + count]
    landed = [scratch[25 + count + s * bits:25 + count + (s + 1) * bits] for s in range(count)]
    shot_dev, det_dev = raw.shape
    block_rows = PB // shot_count
    groups = shot_count // 2
    me = lax.axis_index("shot")
    my_det = lax.axis_index("det")
    shot_total = float(shot_dev * shot_count)
    inverse = 1.0 / shot_total
    bit = [(me // (1 << b)) % 2 for b in range(bits)]
    partner = [me + (1 - 2 * bit[b]) * (1 << b) for b in range(bits)]
    mesh_id = pl.DeviceIdType.MESH

    chunk = shot_dev // load_chunks
    copies = []
    for c in range(load_chunks):
        copy = pltpu.make_async_copy(
            events_ref.at[pl.ds(c * chunk, chunk), :], raw.at[pl.ds(c * chunk, chunk), :], in_sem.at[c])
        copy.start()
        copies.append(copy)
    barrier = pltpu.get_barrier_semaphore()
    for b in range(2):
        pl.semaphore_signal(barrier, inc=1, device_id={"shot": partner[b]}, device_id_type=mesh_id)
    has_up, has_down = me + 4 < shot_count, me >= 4

    def signal_line(sem):
        @pl.when(has_up)
        def _():
            pl.semaphore_signal(sem, inc=1, device_id={"shot": me + 4}, device_id_type=mesh_id)

        @pl.when(has_down)
        def _():
            pl.semaphore_signal(sem, inc=1, device_id={"shot": me - 4}, device_id_type=mesh_id)

    signal_line(barrier)
    line_count = has_up.astype(jnp.int32) + has_down.astype(jnp.int32)
    for d in range(1, det_count):
        pl.semaphore_signal(barrier, inc=1, device_id={"det": (my_det + d) % det_count}, device_id_type=mesh_id)

    def make_slot_table():
        lanes = 128
        lane = lax.broadcasted_iota(jnp.int32, (shot_count, lanes), 1)
        owner = lax.broadcasted_iota(jnp.int32, (shot_count, lanes), 0)
        slot_vector[...] = jnp.full((shot_count, lanes), -1, jnp.int32)
        slot_vector[0:2, 0:pair_count] = owner_ref[...]
        hit_first = (slot_vector[0:1, :] == owner).astype(jnp.int32)
        hit_second = (slot_vector[1:2, :] == owner).astype(jnp.int32)
        both = hit_first + hit_second
        upto = both
        shift = 1
        while shift < pair_count:
            upto = upto + jnp.where(lane >= shift, pltpu.roll(upto, shift, 1), 0)
            shift *= 2
        rank_first = upto - both
        rank_second = rank_first + hit_first
        table = jnp.zeros((shot_count, lanes), jnp.int32)
        for j in range(recv_slots):
            pick = (jnp.where(rank_first == j, hit_first, 0) + jnp.where(rank_second == j, hit_second, 0))
            index = pair_count + jnp.sum(pick * (lane - pair_count), axis=1, keepdims=True)
            table = jnp.where(lane == j, index, table)
        slot_vector[...] = table
        copy = pltpu.make_async_copy(slot_vector, slot_table, table_sem)
        copy.start()
        return copy

    for c in range(load_chunks):
        copies[c].wait()
        piece = raw[pl.ds(c * chunk, chunk), :].astype(jnp.float32).astype(jnp.bfloat16)
        turned[:, :, pl.ds(c * chunk, chunk)] = piece.T.reshape(patch_dev, PB, chunk)

    nt = (((1,), (1,)), ((), ()))

    def stream_base(s, t):
        dims = streams[s][2]
        base = 0
        for i in range(t):
            base = base + bit[dims[i]] * (1 << (len(dims) - 1 - i))
        return base

    def stream_copy(s, t):
        dims = streams[s][2]
        if t == len(dims):
            source = held[s].at[pl.ds(stream_base(s, t), 1)]
            other = partner[bits - 1]
        else:
            length = 1 << (len(dims) - 1 - t)
            source = held[s].at[pl.ds(stream_base(s, t) + (1 - bit[dims[t]]) * length, length)]
            other = partner[dims[t]]
        return pltpu.make_async_remote_copy(
            src_ref=source, dst_ref=landed[s][t], send_sem=send_sem.at[s, t], recv_sem=recv_sem.at[s, t],
            device_id={"shot": other}, device_id_type=mesh_id)

    def place(dims, g):
        return sum(((g >> dims[i]) & 1) << (len(dims) - 1 - i) for i in range(len(dims)))

    def put_intra(s):
        _, _, dims, start, size = streams[s]
        for k in range(size):
            block = turned[start + k]
            gram = lax.dot_general(block, block, nt, preferred_element_type=jnp.float32)
            for g in range(shot_count):
                held[s][place(dims, g), k] = gram[g * block_rows:(g + 1) * block_rows]

    def put_pairs(members):
        _, _, dims, start, size = streams[members[0]]

        @pl.loop(0, size, unroll=True)
        def _(k):
            gram = lax.dot_general(turned[ends_ref[0, start + k]], turned[ends_ref[1, start + k]], nt,
                                   preferred_element_type=jnp.float32)
            for g in range(groups):
                for i, s in enumerate(members):
                    row = (g * tiles + i) * block_rows
                    held[s][place(dims, g), k] = gram[row:row + block_rows]

    put_pairs((PAIR_A0, PAIR_A1))
    pl.semaphore_wait(barrier, 2 + line_count + det_count - 1)
    signal_line(relay)
    stream_copy(PAIR_A0, 0).start()
    put_pairs((PAIR_B0, PAIR_B1))
    stream_copy(PAIR_B0, 0).start()
    for s in (DEEP, SIDE_X, SIDE_Y):
        put_intra(s)
        stream_copy(s, 0).start()
    slot_copy = make_slot_table()

    ones = jnp.ones((8, shot_dev), jnp.bfloat16)
    for p in range(patch_dev):
        total = lax.dot_general(ones, turned[p], nt, preferred_element_type=jnp.float32)
        aux[0, pl.ds(p, 1), :] = total[0:1]
    lane = lax.broadcasted_iota(jnp.int32, (PB, 128), 1)
    for c in range(triple_count // 128):
        column = lax.broadcasted_iota(jnp.int32, (128, det_dev), 1)
        bit_rows = []
        for m in range(3):
            named = jnp.broadcast_to(triple_ref[m, :, pl.ds(c * 128, 128)], (128, 128)).T[:, 0:1]
            bit_rows.append(
                jnp.dot((named == column).astype(jnp.float32).astype(jnp.bfloat16),
                        turned[...].reshape(det_dev, shot_dev), preferred_element_type=jnp.float32))
        one, two, three = bit_rows
        both = one * two
        terms = [one, two, three, both, one * three, two * three, both * three]
        packed = jnp.zeros((128, 128), jnp.float32)
        for q, term in enumerate(terms):
            packed = jnp.where(lane == q, jnp.sum(term, axis=1, keepdims=True), packed)
        aux[0, pl.ds(patch_dev + 8 * c, 8), :] = packed.T[0:8]

    pl.semaphore_wait(relay, line_count)

    def aux_copy(t):
        return pltpu.make_async_remote_copy(
            src_ref=aux.at[t], dst_ref=aux_in.at[t], send_sem=aux_send.at[t], recv_sem=aux_recv.at[t],
            device_id={"shot": partner[t]}, device_id_type=mesh_id)

    aux_copy(0).start()
    slot_copy.wait()

    def step(s, t):
        kind, tile, dims, start, size = streams[s]
        depth = len(dims)
        stream_copy(s, t).wait_recv()
        base = stream_base(s, min(t + 1, depth))
        if t == depth:
            pair_sum[tile, pl.ds(start, size)] = held[s][base] + landed[s][t][0]
        elif t == depth - 1 and kind == "intra":
            intra_sum[pl.ds(start, size)] = held[s][base] + landed[s][t][0]
        elif t == depth - 1:
            held[s][base] = held[s][base] + landed[s][t][0]
            stream_copy(s, t + 1).start()
        else:
            half = 1 << (depth - 2 - t)
            away = (1 - bit[dims[t + 1]]) * half
            keep = bit[dims[t + 1]] * half

            @pl.loop(0, half)
            def _(i):
                held[s][base + away + i] = held[s][base + away + i] + landed[s][t][away + i]
            stream_copy(s, t + 1).start()

            @pl.loop(0, half)
            def _(i):
                held[s][base + keep + i] = held[s][base + keep + i] + landed[s][t][keep + i]

    def rates(coincide, row_rate, col_rate):
        joint_rate = coincide * inverse
        denominator = jnp.maximum(1.0 - 2.0 * row_rate - 2.0 * col_rate + 4.0 * joint_rate, 0.25)
        excess = (joint_rate - row_rate * col_rate) / denominator
        return 100.0 * (0.5 - 0.5 * jnp.sqrt(jnp.maximum(1.0 - 4.0 * excess, 0.04)))

    my_group = me % groups

    def tile_row(i):
        return pl.multiple_of((my_group * tiles + i) * block_rows, block_rows)

    def make_means():
        rows = aux[bits]
        turned_counts[...] = jnp.concatenate(
            [rows * inverse, jnp.zeros((PB - rows.shape[0], PB), jnp.float32)], axis=0).T
        starts = [tile_row(i) for i in range(tiles)] + [pl.multiple_of(me * block_rows, block_rows)]
        for i, row in enumerate(starts):
            piece = turned_counts[pl.ds(row, block_rows), :]
            for p in range(patch_dev):
                row_buf[i, p] = jnp.broadcast_to(piece[:, p:p + 1], (block_rows, PB))
        for p in range(patch_dev):
            col_buf[p] = jnp.broadcast_to(aux[bits, pl.ds(p, 1), :] * inverse, (block_rows, PB))
        fitted[:, pair_count] = jnp.zeros((tiles, block_rows, PB), jnp.float32)
        for c in range(triple_count // 128):
            sums = aux[bits, pl.ds(patch_dev + 8 * c, 8), :] * inverse
            first, second, third = sums[0:1], sums[1:2], sums[2:3]
            kappa = (sums[6:7] - sums[3:4] * third - sums[4:5] * second - sums[5:6] * first
                     + 2.0 * first * second * third)
            kappa_ref[:, pl.ds(c * 128, 128)] = 1000.0 * kappa

    def out_copy(i, m):
        other = me
        for b in range(bits - 1):
            if (m >> b) & 1:
                other = other + (1 - 2 * bit[b]) * (1 << b)
        return other, pltpu.make_async_remote_copy(
            src_ref=outgoing.at[i, m], dst_ref=boundary_ref.at[:, pl.ds(tile_row(i), block_rows), :],
            send_sem=out_send.at[i, m], recv_sem=out_recv.at[i, m],
            device_id={"shot": other}, device_id_type=mesh_id)

    def route(i):
        @pl.loop(0, pair_count, unroll=True)
        def _(k):
            fitted[i, k] = rates(pair_sum[i, k], row_buf[i, ends_ref[0, k]], col_buf[ends_ref[1, k]])
        for m in reversed(range(1, groups)):
            other, copy = out_copy(i, m)
            for j in range(recv_slots):
                outgoing[i, m, j] = fitted[i, slot_table[other, j]]
            copy.start()
        for j in range(recv_slots):
            boundary_ref[j, pl.ds(tile_row(i), block_rows), :] = fitted[i, slot_table[me, j]]

    def load_copy(d):
        return pltpu.make_async_remote_copy(
            src_ref=load_mine, dst_ref=load_ref.at[my_det], send_sem=load_send.at[d], recv_sem=load_recv.at[d],
            device_id={"det": (my_det + d) % det_count}, device_id_type=mesh_id)

    def finish_intra():
        col = lax.broadcasted_iota(jnp.int32, (block_rows, PB), 1)
        loads = jnp.zeros((block_rows, PB), jnp.float32)
        for p in range(patch_dev):
            fit = rates(intra_sum[p], row_buf[tiles, p], col_buf[p])
            intra_ref[p] = fit
            loads = jnp.where(col == my_det * patch_dev + p, jnp.sum(fit, axis=1, keepdims=True), loads)
        load_mine[...] = loads
        for d in range(1, det_count):
            load_copy(d).start()
        load_ref[my_det] = loads

    for op in ORDER:
        if op == "first":
            stream_copy(PAIR_A1, 0).start()
            stream_copy(PAIR_B1, 0).start()
        elif op == "means":
            make_means()
        elif op == "intra":
            finish_intra()
        elif op[0] == "aux":
            t = op[1]
            aux_copy(t).wait_recv()
            aux[t + 1] = aux[t] + aux_in[t]
            if t < bits - 1:
                aux_copy(t + 1).start()
        elif op[0] == "route":
            route(op[1])
        else:
            step(*op)

    for d in range(1, det_count):
        load_copy(d).wait()
    for i in range(tiles):
        for m in range(1, groups):
            out_copy(i, m)[1].wait()
    for t in range(bits):
        aux_copy(t).wait_send()
        for s in range(count):
            stream_copy(s, t).wait_send()


def local_fused(events, pair_patches, pair_owners, triples, det_count):
    shot_dev, det_dev = events.shape
    shot_count = lax.axis_size("shot")
    bits = shot_count.bit_length() - 1
    patch_dev = det_dev // PB
    block_rows = PB // shot_count
    pair_count = pair_patches.shape[1]
    triple_count = triples.shape[1]
    recv_slots = max(2, 4 * pair_count // shot_count)
    streams = plan_streams(bits, patch_dev, pair_count)
    load_chunks = 4
    tiles = 2
    smem = pl.BlockSpec(memory_space=pltpu.SMEM)
    vmem = pl.BlockSpec(memory_space=pltpu.VMEM)
    plan = (streams, shot_count, det_count, patch_dev, pair_count, triple_count, recv_slots, load_chunks, tiles)
    aux_rows = patch_dev + 8 * (triple_count // 128)
    f32 = jnp.float32
    dma = pltpu.SemaphoreType.DMA
    count = len(streams)
    tile = (block_rows, PB)
    scratch = [
        pltpu.VMEM((shot_dev, det_dev), jnp.int32),
        pltpu.VMEM((patch_dev, PB, shot_dev), jnp.bfloat16),
        pltpu.VMEM((bits + 1, aux_rows, 128), f32),
        pltpu.VMEM((bits, aux_rows, 128), f32),
        pltpu.VMEM((patch_dev, *tile), f32),
        pltpu.VMEM((tiles, pair_count, *tile), f32),
        pltpu.VMEM((PB, PB), f32),
        pltpu.VMEM((tiles + 1, patch_dev, *tile), f32),
        pltpu.VMEM((patch_dev, *tile), f32),
        pltpu.VMEM((tiles, pair_count + 1, *tile), f32),
        pltpu.VMEM((tiles, shot_count // 2, recv_slots, *tile), f32),
        pltpu.VMEM(tile, f32),
        pltpu.VMEM((shot_count, 128), jnp.int32),
        pltpu.SMEM((shot_count, 128), jnp.int32),
        dma((load_chunks,)), dma((count, bits)), dma((count, bits)), dma((bits,)), dma((bits,)),
        dma((tiles, shot_count // 2)), dma((tiles, shot_count // 2)), dma((det_count,)), dma((det_count,)),
        pltpu.SemaphoreType.REGULAR, dma,
    ]
    scratch += [pltpu.VMEM((1 << len(dims), size, *tile), f32) for _, _, dims, _, size in streams]
    for _, _, dims, _, size in streams:
        scratch += [pltpu.VMEM((max(1, (1 << len(dims)) >> (t + 1)), size, *tile), f32) for t in range(bits)]
    intra, boundary, load, kappa = pl.pallas_call(
        functools.partial(fused_kernel, plan),
        out_shape=(
            jax.ShapeDtypeStruct((patch_dev, block_rows, PB), f32),
            jax.ShapeDtypeStruct((recv_slots, PB, PB), f32),
            jax.ShapeDtypeStruct((det_count, block_rows, PB), f32),
            jax.ShapeDtypeStruct((1, triple_count), f32),
        ),
        in_specs=[pl.BlockSpec(memory_space=pltpu.HBM), smem, vmem, vmem],
        out_specs=(vmem, vmem, vmem, vmem),
        scratch_shapes=scratch,
        compiler_params=pltpu.CompilerParams(
            collective_id=0, has_side_effects=True, vmem_limit_bytes=58 * 1024 * 1024),
    )(events, jnp.swapaxes(pair_patches[0], 0, 1), jnp.swapaxes(pair_owners[0], 0, 1), jnp.transpose(triples, (2, 0, 1)))
    hbm = pl.BlockSpec(memory_space=pltpu.HBM)
    intra, boundary, load, kappa = pl.pallas_call(
        finish_kernel,
        out_shape=(
            jax.ShapeDtypeStruct((patch_dev, block_rows, PB), f32),
            jax.ShapeDtypeStruct((recv_slots, PB, PB), f32),
            jax.ShapeDtypeStruct((block_rows, det_count * patch_dev), f32),
            jax.ShapeDtypeStruct((1, triple_count), f32),
        ),
        in_specs=[hbm, hbm, hbm, hbm],
        out_specs=(hbm, hbm, vmem, vmem),
        scratch_shapes=[
            pltpu.VMEM((patch_dev, block_rows, PB), f32),
            pltpu.VMEM((recv_slots, PB, PB), f32),
            pltpu.VMEM((det_count, block_rows, PB), f32),
            pltpu.VMEM((1, triple_count), f32),
            dma((5,)), dma((3,)),
        ],
        compiler_params=pltpu.CompilerParams(vmem_limit_bytes=61 * 1024 * 1024),
    )(intra, boundary, load, kappa)
    return (intra, boundary[None, None], jnp.swapaxes(load, 0, 1), kappa)


def local(events, pair_patches, pair_owners, triples):
    shot_dev, det_dev = events.shape
    shot_count = lax.axis_size("shot")
    shot_index = lax.axis_index("shot")
    shot_total = float(shot_dev * shot_count)
    inverse = 1.0 / shot_total
    patch_dev = det_dev // PB
    rows_own = PB // shot_count
    pair_count = pair_patches.shape[1]
    triple_count = triples.shape[1]
    recv_slots = max(2, 4 * pair_count // shot_count)
    bit_matrix = events.astype(jnp.bfloat16)
    patches = bit_matrix.reshape(shot_dev, patch_dev, PB)
    local_counts = jnp.sum(events, axis=0).astype(jnp.float32)
    triple_index = triples[0]
    picked = (
        jnp.take(events, triple_index.reshape(-1), axis=1)
        .astype(jnp.float32)
        .reshape(shot_dev, triple_count, 3)
    )
    first_bit = picked[:, :, 0]
    second_bit = picked[:, :, 1]
    third_bit = picked[:, :, 2]
    triple_terms = jnp.stack(
        [
            jnp.sum(first_bit * second_bit, axis=0),
            jnp.sum(first_bit * third_bit, axis=0),
            jnp.sum(second_bit * third_bit, axis=0),
            jnp.sum(first_bit * second_bit * third_bit, axis=0),
        ]
    )
    intra = jnp.einsum("sai,saj->aij", patches, patches, preferred_element_type=jnp.float32)
    pair_ends = pair_patches[0]

    def pair_gram(ends):
        first = lax.dynamic_slice_in_dim(bit_matrix, ends[0] * PB, PB, 1)
        second = lax.dynamic_slice_in_dim(bit_matrix, ends[1] * PB, PB, 1)
        return lax.dot_general(first, second, (((0,), (0,)), ((), ())), preferred_element_type=jnp.float32)

    cross = lax.map(pair_gram, pair_ends)
    joined = lax.psum_scatter(
        jnp.concatenate([intra, cross], axis=0), "shot", scatter_dimension=1, tiled=True
    )
    intra_share = joined[:patch_dev]
    pair_share = joined[patch_dev:]
    counts, triple_total = lax.psum((local_counts, triple_terms), "shot")
    patch_counts = counts.reshape(patch_dev, PB)
    row_counts = lax.dynamic_slice_in_dim(patch_counts, shot_index * rows_own, rows_own, 1)
    intra_rates = fit_rates(intra_share, row_counts, patch_counts, shot_total)
    load_share = jnp.sum(intra_rates, axis=2)
    detector_load = lax.all_gather(load_share, "det", axis=0, tiled=True)
    pair_slot, valid = route_table(pair_owners[0].reshape(-1), shot_count, recv_slots)
    mine = lax.dynamic_index_in_dim(pair_slot, shot_index, 0, keepdims=False)
    valid_mine = lax.dynamic_index_in_dim(valid, shot_index, 0, keepdims=False)
    fitted = fit_rates(
        pair_share,
        jnp.take(row_counts, pair_ends[:, 0], axis=0),
        jnp.take(patch_counts, pair_ends[:, 1], axis=0),
        shot_total,
    )
    every_block = lax.all_gather(fitted, "shot", axis=1, tiled=True)
    boundary = lax.map(lambda k: lax.dynamic_index_in_dim(every_block, k, 0, keepdims=False), mine)
    boundary = boundary * valid_mine[:, None, None]
    moments = triple_total * inverse
    means = jnp.take(counts, triple_index.reshape(-1), axis=0).reshape(triple_count, 3) * inverse
    mean_first = means[:, 0]
    mean_second = means[:, 1]
    mean_third = means[:, 2]
    kappa = (
        moments[3]
        - moments[0] * mean_third
        - moments[1] * mean_second
        - moments[2] * mean_first
        + 2.0 * mean_first * mean_second * mean_third
    )
    triple_cumulant = 1000.0 * kappa
    return (intra_rates, boundary[None, None], detector_load, triple_cumulant[None])


def solution(mesh):
    placed = (P("shot", "det"), P("det", None, None), P("det", None, None), P("det", None, None))
    shot_count = mesh.shape["shot"]
    det_count = mesh.shape["det"]
    power_of_two = shot_count & (shot_count - 1) == 0 and shot_count > 1
    whole_tiles = PB % shot_count == 0 and (PB // shot_count) % 8 == 0

    def body(events, pair_patches, pair_owners, triples):
        if power_of_two and whole_tiles and shot_count > 8 and triples.shape[1] % 128 == 0:
            return local_fused(events, pair_patches, pair_owners, triples, det_count)
        return local(events, pair_patches, pair_owners, triples)

    return jax.shard_map(
        body,
        mesh=mesh,
        in_specs=placed,
        out_specs=(
            P("det", "shot", None),
            P("det", "shot", None, None, None),
            P(None, "shot"),
            P("det", None),
        ),
        check_vma=False,
    )
```

```python
import functools

import jax
import jax.numpy as jnp
from jax import lax
from jax.experimental import pallas as pl
from jax.experimental.pallas import tpu as pltpu
from jax.sharding import PartitionSpec as P

PB = 128
VMEM_BYTES = 52 * 1024 * 1024


def fit_rates(coincide, row_count, col_count, shot_total):
    inverse = 1.0 / shot_total
    joint_rate = coincide * inverse
    row_rate = row_count[..., :, None] * inverse
    col_rate = col_count[..., None, :] * inverse
    denominator = jnp.maximum(1.0 - 2.0 * row_rate - 2.0 * col_rate + 4.0 * joint_rate, 0.25)
    excess = (joint_rate - row_rate * col_rate) / denominator
    return 100.0 * (0.5 - 0.5 * jnp.sqrt(jnp.maximum(1.0 - 4.0 * excess, 0.04)))


def route_table(owner_row, shot_count, recv_slots):
    owner_ids = jnp.arange(shot_count, dtype=jnp.int32)
    hit = owner_row[None, :] == owner_ids[:, None]
    entry_ids = jnp.arange(owner_row.shape[0], dtype=jnp.int32)
    upto = entry_ids[:, None] >= entry_ids[None, :]
    rank = jnp.sum(jnp.where(hit[:, None, :] & upto[None, :, :], 1, 0), axis=2) - 1
    slot_ids = jnp.arange(recv_slots, dtype=jnp.int32)
    chosen = hit[:, None, :] & (rank[:, None, :] == slot_ids[None, :, None])
    entry_pair = jnp.arange(owner_row.shape[0], dtype=jnp.int32) // 2
    pair_slot = jnp.sum(jnp.where(chosen, entry_pair[None, None, :], 0), axis=2)
    valid = jnp.any(chosen, axis=2).astype(jnp.float32)
    return (pair_slot, valid)


STREAMS = [
    ('pair', 0, (2, 1, 0), 4), ('pair', 0, (1, 0, 2), 6), ('pair', 0, (0, 1, 2), 8), ('pair', 0, (0, 1, 2), 8),
    ('pair', 1, (1, 0, 2), 9), ('pair', 1, (2, 0, 1), 5), ('pair', 1, (1, 2, 0), 5), ('pair', 1, (0, 1, 2), 7),
    ('intra', 0, (2, 1, 0, 3), 2), ('intra', 0, (2, 1, 0, 3), 3), ('intra', 0, (2, 1, 0, 3), 3),
]
ORDER = [
    ('start', 0), ('start', 1), ('start', 3), ('start', 8), ('start', 9), ('start', 6), ('start', 4), ('start', 10),
    ('start', 2), (1, 0), (3, 0), (0, 0), (6, 0), ('start', 5), ('start', 7), (2, 0), (4, 0), (1, 1), ('aux', 0),
    (3, 1), (6, 1), (8, 0), (5, 0), (7, 0), (1, 2), (2, 1), (0, 1), (3, 2), (9, 0), ('aux', 1), (6, 2), (10, 0), (4, 1),
    (5, 1), (7, 1), (2, 2), (0, 2), (9, 1), ('aux', 2), (10, 1), (8, 1), (4, 2), (5, 2), (0, 3), (7, 2), (10, 2),
    (1, 3), (6, 3), (2, 3), ('aux', 3), (8, 2), (3, 3), ('route', 0), (5, 3), (9, 2), (4, 3), (7, 3), ('route', 1),
    (8, 3), (10, 3), (9, 3), 'intra',
]


def plan_streams(patch_dev, pair_count):
    streams = [None] * len(STREAMS)
    for kind in (("pair", 0), ("pair", 1), ("intra", 0)):
        total = pair_count if kind[0] == "pair" else patch_dev
        members = [s for s, stream in enumerate(STREAMS) if stream[:2] == kind]
        whole = sum(STREAMS[s][3] for s in members)
        start, seen = 0, 0
        for s in members:
            seen += STREAMS[s][3]
            stop = total * seen // whole
            streams[s] = (*STREAMS[s][:3], start, stop - start)
            start = stop
    return streams


def finish_kernel(patch_dev, det_count, packed_in, intra_out, boundary_out, load_out, kappa_out, out_sem):
    slots = boundary_out.shape[0]
    rows = intra_out.shape[0]
    leave = [pltpu.make_async_copy(packed_in.at[pl.ds(0, slots)], boundary_out, out_sem.at[0]),
             pltpu.make_async_copy(packed_in.at[slots, pl.ds(0, rows)], intra_out, out_sem.at[1])]
    for copy in leave:
        copy.start()
    height = rows // patch_dev
    total = packed_in[slots, rows:rows + height]
    for d in range(1, det_count):
        total = total + packed_in[slots, rows + d * height:rows + (d + 1) * height]
    load_out[...] = total[:, 0:load_out.shape[1]]
    first = rows + det_count * height
    for c in range(kappa_out.shape[1] // PB):
        kappa_out[:, pl.ds(c * PB, PB)] = packed_in[slots, first + c:first + c + 1]
    for copy in leave:
        copy.wait()


def fused_kernel(plan, events_ref, ends_ref, tables_ref, packed_ref, *scratch):
    (streams, shot_count, det_count, patch_dev, pair_count, triple_count, recv_slots, load_chunks, tiles) = plan
    bits = shot_count.bit_length() - 1
    count = len(streams)
    raw, turned, aux, aux_in, intra_sum, pair_sum, turned_counts, row_buf, col_buf, fitted, outgoing, load_mine = scratch[:12]
    slot_vector, slot_table = scratch[12:14]
    (in_sem, send_sem, recv_sem, aux_send, aux_recv, out_send, out_recv, load_send, load_recv, relay,
     table_sem) = scratch[14:25]
    held = scratch[25:25 + count]
    landed = [scratch[25 + count + s * bits:25 + count + (s + 1) * bits] for s in range(count)]
    shot_dev, det_dev = raw.shape
    block_rows = PB // shot_count
    groups = shot_count // 2
    me = lax.axis_index("shot")
    my_det = lax.axis_index("det")
    shot_total = float(shot_dev * shot_count)
    inverse = 1.0 / shot_total
    bit = [(me // (1 << b)) % 2 for b in range(bits)]
    partner = [me + (1 - 2 * bit[b]) * (1 << b) for b in range(bits)]
    mesh_id = pl.DeviceIdType.MESH

    chunk = shot_dev // load_chunks
    copies = []
    for c in range(load_chunks):
        copy = pltpu.make_async_copy(
            events_ref.at[pl.ds(c * chunk, chunk), :], raw.at[pl.ds(c * chunk, chunk), :], in_sem.at[c])
        copy.start()
        copies.append(copy)
    barrier = pltpu.get_barrier_semaphore()
    for b in range(2):
        pl.semaphore_signal(barrier, inc=1, device_id={"shot": partner[b]}, device_id_type=mesh_id)
    has_up, has_down = me + 4 < shot_count, me >= 4

    def signal_line(sem):
        @pl.when(has_up)
        def _():
            pl.semaphore_signal(sem, inc=1, device_id={"shot": me + 4}, device_id_type=mesh_id)

        @pl.when(has_down)
        def _():
            pl.semaphore_signal(sem, inc=1, device_id={"shot": me - 4}, device_id_type=mesh_id)

    signal_line(barrier)
    line_count = has_up.astype(jnp.int32) + has_down.astype(jnp.int32)
    for d in range(1, det_count):
        pl.semaphore_signal(barrier, inc=1, device_id={"det": (my_det + d) % det_count}, device_id_type=mesh_id)

    def make_slot_table():
        lanes = 128
        lane = lax.broadcasted_iota(jnp.int32, (shot_count, lanes), 1)
        owner = lax.broadcasted_iota(jnp.int32, (shot_count, lanes), 0)
        hit_first = (tables_ref[2, :, 0:lanes] == owner).astype(jnp.int32)
        hit_second = (tables_ref[3, :, 0:lanes] == owner).astype(jnp.int32)
        both = hit_first + hit_second
        upto = both
        shift = 1
        while shift < pair_count:
            upto = upto + jnp.where(lane >= shift, pltpu.roll(upto, shift, 1), 0)
            shift *= 2
        rank_first = upto - both
        rank_second = rank_first + hit_first
        table = jnp.zeros((shot_count, lanes), jnp.int32)
        for j in range(recv_slots):
            pick = (jnp.where(rank_first == j, hit_first, 0) + jnp.where(rank_second == j, hit_second, 0))
            index = pair_count + jnp.sum(pick * (lane - pair_count), axis=1, keepdims=True)
            table = jnp.where(lane == j, index, table)
        slot_vector[...] = table
        copy = pltpu.make_async_copy(slot_vector, slot_table, table_sem)
        copy.start()
        return copy

    for c in range(load_chunks):
        copies[c].wait()
        piece = raw[pl.ds(c * chunk, chunk), :].astype(jnp.float32).astype(jnp.bfloat16)
        turned[:, :, pl.ds(c * chunk, chunk)] = piece.T.reshape(patch_dev, PB, chunk)

    nt = (((1,), (1,)), ((), ()))

    def stream_base(s, t):
        dims = streams[s][2]
        base = 0
        for i in range(t):
            base = base + bit[dims[i]] * (1 << (len(dims) - 1 - i))
        return base

    def stream_copy(s, t):
        dims = streams[s][2]
        if t == len(dims):
            source = held[s].at[pl.ds(stream_base(s, t), 1)]
            other = partner[bits - 1]
        else:
            length = 1 << (len(dims) - 1 - t)
            source = held[s].at[pl.ds(stream_base(s, t) + (1 - bit[dims[t]]) * length, length)]
            other = partner[dims[t]]
        return pltpu.make_async_remote_copy(
            src_ref=source, dst_ref=landed[s][t], send_sem=send_sem.at[s, t], recv_sem=recv_sem.at[s, t],
            device_id={"shot": other}, device_id_type=mesh_id)

    def place(dims, g):
        return sum(((g >> dims[i]) & 1) << (len(dims) - 1 - i) for i in range(len(dims)))

    owner_of = {}
    for s, (kind, tile, _, start, size) in enumerate(streams):
        for k in range(size):
            owner_of[kind, tile, start + k] = (s, k)
    done = set()

    def put(s):
        kind, _, _, start, size = streams[s]
        for k in range(start, start + size):
            if (kind, k) in done:
                continue
            done.add((kind, k))
            if kind == "intra":
                left, right = turned[k], turned[k]
            else:
                left, right = turned[ends_ref[0, 0, k]], turned[ends_ref[1, 0, k]]
            gram = lax.dot_general(left, right, nt, preferred_element_type=jnp.float32)
            if kind == "intra":
                where = [(0, g, g) for g in range(shot_count)]
            else:
                where = [(i, g, i * groups + g) for i in range(tiles) for g in range(groups)]
            for i, g, row in where:
                to, at = owner_of[kind, i, k]
                held[to][place(streams[to][2], g), at] = gram[row * block_rows:(row + 1) * block_rows]

    lead = []
    for op in ORDER:
        if op[0] != "start":
            break
        lead.append(op[1])
    for n, s in enumerate(lead):
        put(s)
        if n == 0:
            pl.semaphore_wait(barrier, 2 + line_count + det_count - 1)
            signal_line(relay)
        stream_copy(s, 0).start()
    for s in range(count):
        put(s)
    slot_copy = make_slot_table()

    ones = jnp.ones((8, shot_dev), jnp.bfloat16)
    for p in range(patch_dev):
        total = lax.dot_general(ones, turned[p], nt, preferred_element_type=jnp.float32)
        aux[0, pl.ds(p, 1), :] = total[0:1]
    lane = lax.broadcasted_iota(jnp.int32, (PB, 128), 1)
    for c in range(triple_count // 128):
        column = lax.broadcasted_iota(jnp.int32, (128, det_dev), 1)
        bit_rows = []
        for m in range(3):
            named = jnp.broadcast_to(tables_ref[4 + m, :, pl.ds(c * 128, 128)], (128, 128)).T[:, 0:1]
            bit_rows.append(
                jnp.dot((named == column).astype(jnp.float32).astype(jnp.bfloat16),
                        turned[...].reshape(det_dev, shot_dev), preferred_element_type=jnp.float32))
        one, two, three = bit_rows
        both = one * two
        terms = [one, two, three, both, one * three, two * three, both * three]
        packed = jnp.zeros((128, 128), jnp.float32)
        for q, term in enumerate(terms):
            packed = jnp.where(lane == q, jnp.sum(term, axis=1, keepdims=True), packed)
        aux[0, pl.ds(patch_dev + 8 * c, 8), :] = packed.T[0:8]

    pl.semaphore_wait(relay, line_count)

    def aux_copy(t):
        return pltpu.make_async_remote_copy(
            src_ref=aux.at[t], dst_ref=aux_in.at[t], send_sem=aux_send.at[t], recv_sem=aux_recv.at[t],
            device_id={"shot": partner[t]}, device_id_type=mesh_id)

    aux_copy(0).start()
    slot_copy.wait()

    def step(s, t):
        kind, tile, dims, start, size = streams[s]
        depth = len(dims)
        stream_copy(s, t).wait_recv()
        base = stream_base(s, min(t + 1, depth))
        if t == depth:
            pair_sum[tile, pl.ds(start, size)] = held[s][base] + landed[s][t][0]
        elif t == depth - 1 and kind == "intra":
            intra_sum[pl.ds(start, size)] = held[s][base] + landed[s][t][0]
        elif t == depth - 1:
            held[s][base] = held[s][base] + landed[s][t][0]
            stream_copy(s, t + 1).start()
        else:
            half = 1 << (depth - 2 - t)
            away = (1 - bit[dims[t + 1]]) * half
            keep = bit[dims[t + 1]] * half

            def add(part):
                mine = pl.ds(base + part, half)
                held[s][mine] = held[s][mine] + landed[s][t][pl.ds(part, half)]
            add(away)
            stream_copy(s, t + 1).start()
            add(keep)

    def rates(coincide, row_rate, col_rate):
        joint_rate = coincide * inverse
        denominator = jnp.maximum(1.0 - 2.0 * row_rate - 2.0 * col_rate + 4.0 * joint_rate, 0.25)
        excess = (joint_rate - row_rate * col_rate) / denominator
        return 100.0 * (0.5 - 0.5 * jnp.sqrt(jnp.maximum(1.0 - 4.0 * excess, 0.04)))

    my_group = me % groups

    def tile_row(i):
        return pl.multiple_of((i * groups + my_group) * block_rows, block_rows)

    def make_means():
        rows = aux[bits]
        turned_counts[...] = jnp.concatenate(
            [rows * inverse, jnp.zeros((PB - rows.shape[0], PB), jnp.float32)], axis=0).T
        starts = [tile_row(i) for i in range(tiles)] + [pl.multiple_of(me * block_rows, block_rows)]
        for i, row in enumerate(starts):
            piece = turned_counts[pl.ds(row, block_rows), :]
            for p in range(patch_dev):
                row_buf[i, p] = jnp.broadcast_to(piece[:, p:p + 1], (block_rows, PB))
        for p in range(patch_dev):
            col_buf[p] = jnp.broadcast_to(aux[bits, pl.ds(p, 1), :] * inverse, (block_rows, PB))
        fitted[:, pair_count] = jnp.zeros((tiles, block_rows, PB), jnp.float32)
        for c in range(triple_count // 128):
            sums = aux[bits, pl.ds(patch_dev + 8 * c, 8), :] * inverse
            first, second, third = sums[0:1], sums[1:2], sums[2:3]
            kappa = (sums[6:7] - sums[3:4] * third - sums[4:5] * second - sums[5:6] * first
                     + 2.0 * first * second * third)
            row = (patch_dev + det_count) * block_rows + c
            packed_ref[recv_slots, row:row + 1, :] = 1000.0 * kappa

    def out_copy(i, m):
        other = me
        for b in range(bits - 1):
            if (m >> b) & 1:
                other = other + (1 - 2 * bit[b]) * (1 << b)
        return other, pltpu.make_async_remote_copy(
            src_ref=outgoing.at[i, m], dst_ref=packed_ref.at[pl.ds(0, recv_slots), pl.ds(tile_row(i), block_rows), :],
            send_sem=out_send.at[i, m], recv_sem=out_recv.at[i, m],
            device_id={"shot": other}, device_id_type=mesh_id)

    def route(i):
        @pl.loop(0, pair_count, unroll=True)
        def _(k):
            fitted[i, k] = rates(pair_sum[i, k], row_buf[i, ends_ref[0, 0, k]], col_buf[ends_ref[1, 0, k]])
        for m in reversed(range(1, groups)):
            other, copy = out_copy(i, m)
            for j in range(recv_slots):
                outgoing[i, m, j] = fitted[i, slot_table[other, j]]
            copy.start()
        for j in range(recv_slots):
            packed_ref[j, pl.ds(tile_row(i), block_rows), :] = fitted[i, slot_table[me, j]]

    load_rows = pl.ds(pl.multiple_of((patch_dev + my_det) * block_rows, block_rows), block_rows)

    def load_copy(d):
        return pltpu.make_async_remote_copy(
            src_ref=load_mine, dst_ref=packed_ref.at[recv_slots, load_rows, :], send_sem=load_send.at[d], recv_sem=load_recv.at[d],
            device_id={"det": (my_det + d) % det_count}, device_id_type=mesh_id)

    def finish_intra():
        col = lax.broadcasted_iota(jnp.int32, (block_rows, PB), 1)
        loads = jnp.zeros((block_rows, PB), jnp.float32)
        for p in range(patch_dev):
            fit = rates(intra_sum[p], row_buf[tiles, p], col_buf[p])
            packed_ref[recv_slots, p * block_rows:(p + 1) * block_rows, :] = fit
            loads = jnp.where(col == my_det * patch_dev + p, jnp.sum(fit, axis=1, keepdims=True), loads)
        load_mine[...] = loads
        for d in range(1, det_count):
            load_copy(d).start()
        packed_ref[recv_slots, load_rows, :] = loads

    for op in ORDER[len(lead):]:
        if op == "intra":
            finish_intra()
        elif op[0] == "start":
            stream_copy(op[1], 0).start()
        elif op[0] == "aux":
            t = op[1]
            aux_copy(t).wait_recv()
            aux[t + 1] = aux[t] + aux_in[t]
            if t < bits - 1:
                aux_copy(t + 1).start()
            else:
                make_means()
        elif op[0] == "route":
            route(op[1])
        else:
            step(*op)

    for d in range(1, det_count):
        load_copy(d).wait()
    for i in range(tiles):
        for m in range(1, groups):
            out_copy(i, m)[1].wait()
    for t in range(bits):
        aux_copy(t).wait_send()
        for s in range(count):
            stream_copy(s, t).wait_send()


def local_fused(events, pair_patches, pair_owners, triples, det_count):
    shot_dev, det_dev = events.shape
    shot_count = lax.axis_size("shot")
    bits = shot_count.bit_length() - 1
    patch_dev = det_dev // PB
    block_rows = PB // shot_count
    pair_count = pair_patches.shape[1]
    triple_count = triples.shape[1]
    recv_slots = max(2, 4 * pair_count // shot_count)
    streams = plan_streams(patch_dev, pair_count)
    load_chunks = 4
    tiles = 2
    smem = pl.BlockSpec(memory_space=pltpu.SMEM)
    vmem = pl.BlockSpec(memory_space=pltpu.VMEM)
    plan = (streams, shot_count, det_count, patch_dev, pair_count, triple_count, recv_slots, load_chunks, tiles)
    aux_rows = patch_dev + 8 * (triple_count // 128)
    f32 = jnp.float32
    dma = pltpu.SemaphoreType.DMA
    count = len(streams)
    tile = (block_rows, PB)
    scratch = [
        pltpu.VMEM((shot_dev, det_dev), jnp.int32),
        pltpu.VMEM((patch_dev, PB, shot_dev), jnp.bfloat16),
        pltpu.VMEM((bits + 1, aux_rows, 128), f32),
        pltpu.VMEM((bits, aux_rows, 128), f32),
        pltpu.VMEM((patch_dev, *tile), f32),
        pltpu.VMEM((tiles, pair_count, *tile), f32),
        pltpu.VMEM((PB, PB), f32),
        pltpu.VMEM((tiles + 1, patch_dev, *tile), f32),
        pltpu.VMEM((patch_dev, *tile), f32),
        pltpu.VMEM((tiles, pair_count + 1, *tile), f32),
        pltpu.VMEM((tiles, shot_count // 2, recv_slots, *tile), f32),
        pltpu.VMEM(tile, f32),
        pltpu.VMEM((shot_count, 128), jnp.int32),
        pltpu.SMEM((shot_count, 128), jnp.int32),
        dma((load_chunks,)), dma((count, bits)), dma((count, bits)), dma((bits,)), dma((bits,)),
        dma((tiles, shot_count // 2)), dma((tiles, shot_count // 2)), dma((det_count,)), dma((det_count,)),
        pltpu.SemaphoreType.REGULAR, dma,
    ]
    scratch += [pltpu.VMEM((1 << len(dims), size, *tile), f32) for _, _, dims, _, size in streams]
    for _, _, dims, _, size in streams:
        scratch += [pltpu.VMEM((max(1, (1 << len(dims)) >> (t + 1)), size, *tile), f32) for t in range(bits)]
    def lanes(rows, fill):
        rows = jnp.transpose(rows, (2, 0, 1))
        return jnp.pad(rows, ((0, 0), (0, 0), (0, triple_count - pair_count)), constant_values=fill)

    tables = jnp.concatenate(
        [lanes(pair_patches, 0), lanes(pair_owners, -1), jnp.transpose(triples, (2, 0, 1))], axis=0)
    packed = pl.pallas_call(
        functools.partial(fused_kernel, plan),
        out_shape=jax.ShapeDtypeStruct((recv_slots + 1, PB, PB), f32),
        in_specs=[pl.BlockSpec(memory_space=pltpu.HBM), smem, vmem],
        out_specs=vmem,
        scratch_shapes=scratch,
        compiler_params=pltpu.CompilerParams(
            collective_id=0, has_side_effects=True, vmem_limit_bytes=VMEM_BYTES),
    )(events, tables, tables)
    hbm = pl.BlockSpec(memory_space=pltpu.HBM)
    intra, boundary, load, kappa = pl.pallas_call(
        functools.partial(finish_kernel, patch_dev, det_count),
        out_shape=(
            jax.ShapeDtypeStruct((patch_dev * block_rows, PB), f32),
            jax.ShapeDtypeStruct((recv_slots, PB, PB), f32),
            jax.ShapeDtypeStruct((block_rows, det_count * patch_dev), f32),
            jax.ShapeDtypeStruct((1, triple_count), f32),
        ),
        in_specs=[vmem],
        out_specs=(hbm, hbm, vmem, vmem),
        scratch_shapes=[dma((2,))],
        compiler_params=pltpu.CompilerParams(vmem_limit_bytes=4 * 1024 * 1024),
    )(packed)
    return (intra.reshape(patch_dev, block_rows, PB), boundary[None, None], jnp.swapaxes(load, 0, 1), kappa)


def local(events, pair_patches, pair_owners, triples):
    shot_dev, det_dev = events.shape
    shot_count = lax.axis_size("shot")
    shot_index = lax.axis_index("shot")
    shot_total = float(shot_dev * shot_count)
    inverse = 1.0 / shot_total
    patch_dev = det_dev // PB
    rows_own = PB // shot_count
    pair_count = pair_patches.shape[1]
    triple_count = triples.shape[1]
    recv_slots = max(2, 4 * pair_count // shot_count)
    bit_matrix = events.astype(jnp.bfloat16)
    patches = bit_matrix.reshape(shot_dev, patch_dev, PB)
    local_counts = jnp.sum(events, axis=0).astype(jnp.float32)
    triple_index = triples[0]
    picked = (
        jnp.take(events, triple_index.reshape(-1), axis=1)
        .astype(jnp.float32)
        .reshape(shot_dev, triple_count, 3)
    )
    first_bit = picked[:, :, 0]
    second_bit = picked[:, :, 1]
    third_bit = picked[:, :, 2]
    triple_terms = jnp.stack(
        [
            jnp.sum(first_bit * second_bit, axis=0),
            jnp.sum(first_bit * third_bit, axis=0),
            jnp.sum(second_bit * third_bit, axis=0),
            jnp.sum(first_bit * second_bit * third_bit, axis=0),
        ]
    )
    intra = jnp.einsum("sai,saj->aij", patches, patches, preferred_element_type=jnp.float32)
    pair_ends = pair_patches[0]

    def pair_gram(ends):
        first = lax.dynamic_slice_in_dim(bit_matrix, ends[0] * PB, PB, 1)
        second = lax.dynamic_slice_in_dim(bit_matrix, ends[1] * PB, PB, 1)
        return lax.dot_general(first, second, (((0,), (0,)), ((), ())), preferred_element_type=jnp.float32)

    cross = lax.map(pair_gram, pair_ends)
    joined = lax.psum_scatter(
        jnp.concatenate([intra, cross], axis=0), "shot", scatter_dimension=1, tiled=True
    )
    intra_share = joined[:patch_dev]
    pair_share = joined[patch_dev:]
    counts, triple_total = lax.psum((local_counts, triple_terms), "shot")
    patch_counts = counts.reshape(patch_dev, PB)
    row_counts = lax.dynamic_slice_in_dim(patch_counts, shot_index * rows_own, rows_own, 1)
    intra_rates = fit_rates(intra_share, row_counts, patch_counts, shot_total)
    load_share = jnp.sum(intra_rates, axis=2)
    detector_load = lax.all_gather(load_share, "det", axis=0, tiled=True)
    pair_slot, valid = route_table(pair_owners[0].reshape(-1), shot_count, recv_slots)
    mine = lax.dynamic_index_in_dim(pair_slot, shot_index, 0, keepdims=False)
    valid_mine = lax.dynamic_index_in_dim(valid, shot_index, 0, keepdims=False)
    fitted = fit_rates(
        pair_share,
        jnp.take(row_counts, pair_ends[:, 0], axis=0),
        jnp.take(patch_counts, pair_ends[:, 1], axis=0),
        shot_total,
    )
    every_block = lax.all_gather(fitted, "shot", axis=1, tiled=True)
    boundary = lax.map(lambda k: lax.dynamic_index_in_dim(every_block, k, 0, keepdims=False), mine)
    boundary = boundary * valid_mine[:, None, None]
    moments = triple_total * inverse
    means = jnp.take(counts, triple_index.reshape(-1), axis=0).reshape(triple_count, 3) * inverse
    mean_first = means[:, 0]
    mean_second = means[:, 1]
    mean_third = means[:, 2]
    kappa = (
        moments[3]
        - moments[0] * mean_third
        - moments[1] * mean_second
        - moments[2] * mean_first
        + 2.0 * mean_first * mean_second * mean_third
    )
    triple_cumulant = 1000.0 * kappa
    return (intra_rates, boundary[None, None], detector_load, triple_cumulant[None])


def solution(mesh):
    placed = (P("shot", "det"), P("det", None, None), P("det", None, None), P("det", None, None))
    shot_count = mesh.shape["shot"]
    det_count = mesh.shape["det"]
    power_of_two = shot_count & (shot_count - 1) == 0 and shot_count > 1
    whole_tiles = PB % shot_count == 0 and (PB // shot_count) % 8 == 0

    def body(events, pair_patches, pair_owners, triples):
        if power_of_two and whole_tiles and shot_count > 8 and triples.shape[1] % 128 == 0:
            return local_fused(events, pair_patches, pair_owners, triples, det_count)
        return local(events, pair_patches, pair_owners, triples)

    return jax.shard_map(
        body,
        mesh=mesh,
        in_specs=placed,
        out_specs=(
            P("det", "shot", None),
            P("det", "shot", None, None, None),
            P(None, "shot"),
            P("det", None),
        ),
        check_vma=False,
    )
```

```python
import functools

import jax
import jax.numpy as jnp
from jax import lax
from jax.experimental import pallas as pl
from jax.experimental.pallas import tpu as pltpu
from jax.sharding import PartitionSpec as P

PB = 128
VMEM_BYTES = 52 * 1024 * 1024


def fit_rates(coincide, row_count, col_count, shot_total):
    inverse = 1.0 / shot_total
    joint_rate = coincide * inverse
    row_rate = row_count[..., :, None] * inverse
    col_rate = col_count[..., None, :] * inverse
    denominator = jnp.maximum(1.0 - 2.0 * row_rate - 2.0 * col_rate + 4.0 * joint_rate, 0.25)
    excess = (joint_rate - row_rate * col_rate) / denominator
    return 100.0 * (0.5 - 0.5 * jnp.sqrt(jnp.maximum(1.0 - 4.0 * excess, 0.04)))


def route_table(owner_row, shot_count, recv_slots):
    owner_ids = jnp.arange(shot_count, dtype=jnp.int32)
    hit = owner_row[None, :] == owner_ids[:, None]
    entry_ids = jnp.arange(owner_row.shape[0], dtype=jnp.int32)
    upto = entry_ids[:, None] >= entry_ids[None, :]
    rank = jnp.sum(jnp.where(hit[:, None, :] & upto[None, :, :], 1, 0), axis=2) - 1
    slot_ids = jnp.arange(recv_slots, dtype=jnp.int32)
    chosen = hit[:, None, :] & (rank[:, None, :] == slot_ids[None, :, None])
    entry_pair = jnp.arange(owner_row.shape[0], dtype=jnp.int32) // 2
    pair_slot = jnp.sum(jnp.where(chosen, entry_pair[None, None, :], 0), axis=2)
    valid = jnp.any(chosen, axis=2).astype(jnp.float32)
    return (pair_slot, valid)


STREAMS = [
    ('pair', 0, (0, 1, 2), 4), ('pair', 0, (2, 1, 0), 6), ('pair', 0, (0, 1, 2), 9), ('pair', 0, (2, 0, 1), 7),
    ('pair', 1, (1, 2, 0), 5), ('pair', 1, (2, 1, 0), 7), ('pair', 1, (1, 0, 2), 7), ('pair', 1, (0, 1, 2), 7),
    ('intra', 0, (2, 0, 1, 3), 2), ('intra', 0, (1, 0, 2, 3), 4), ('intra', 0, (2, 0, 1, 3), 2),
]
ORDER = [
    ('start', 5), ('start', 0), ('start', 4), ('start', 7), ('start', 6), ('start', 2), ('start', 3), ('triples', 1),
    (0, 0), (4, 0), ('start', 10), ('start', 1), (5, 0), ('triples', 0), (7, 0), ('counts',), ('start', 8), (6, 0),
    ('start', 9), (0, 1), (4, 1), (5, 1), (3, 0), ('aux', 0), (2, 0), (7, 1), (4, 2), (10, 0), (1, 0), (6, 1), (5, 2),
    (8, 0), ('aux', 1), (9, 0), (0, 2), (3, 1), (7, 2), (2, 1), (4, 3), (6, 2), (10, 1), ('aux', 2), (1, 1), (3, 2),
    (8, 1), (9, 1), (2, 2), (6, 3), (5, 3), (7, 3), (1, 2), (8, 2), ('aux', 3), ('route', 1), (9, 2), (10, 2), (0, 3),
    (3, 3), (2, 3), (1, 3), ('route', 0), (10, 3), (8, 3), (9, 3), ('intra',),
]


def plan_streams(patch_dev, pair_count):
    streams = [None] * len(STREAMS)
    for kind in (("pair", 0), ("pair", 1), ("intra", 0)):
        total = pair_count if kind[0] == "pair" else patch_dev
        members = [s for s, stream in enumerate(STREAMS) if stream[:2] == kind]
        whole = sum(STREAMS[s][3] for s in members)
        start, seen = 0, 0
        for s in members:
            seen += STREAMS[s][3]
            stop = total * seen // whole
            streams[s] = (*STREAMS[s][:3], start, stop - start)
            start = stop
    return streams


def finish_kernel(patch_dev, det_count, packed_in, intra_out, boundary_out, load_out, kappa_out, out_sem):
    slots = boundary_out.shape[0]
    rows = intra_out.shape[0]
    leave = [pltpu.make_async_copy(packed_in.at[pl.ds(0, slots)], boundary_out, out_sem.at[0]),
             pltpu.make_async_copy(packed_in.at[slots, pl.ds(0, rows)], intra_out, out_sem.at[1])]
    for copy in leave:
        copy.start()
    height = rows // patch_dev
    total = packed_in[slots, rows:rows + height]
    for d in range(1, det_count):
        total = total + packed_in[slots, rows + d * height:rows + (d + 1) * height]
    load_out[...] = total[:, 0:load_out.shape[1]]
    first = rows + det_count * height
    for c in range(kappa_out.shape[1] // PB):
        kappa_out[:, pl.ds(c * PB, PB)] = packed_in[slots, first + c:first + c + 1]
    for copy in leave:
        copy.wait()


def fused_kernel(plan, events_ref, ends_ref, tables_ref, packed_ref, *scratch):
    (streams, shot_count, det_count, patch_dev, pair_count, triple_count, recv_slots, load_chunks, tiles) = plan
    bits = shot_count.bit_length() - 1
    count = len(streams)
    raw, turned, aux, aux_in, intra_sum, pair_sum, turned_counts, row_buf, col_buf, fitted, outgoing, load_mine = scratch[:12]
    slot_vector, slot_table = scratch[12:14]
    (in_sem, send_sem, recv_sem, aux_send, aux_recv, out_send, out_recv, load_send, load_recv, relay,
     table_sem) = scratch[14:25]
    held = scratch[25:25 + count]
    landed = [scratch[25 + count + s * bits:25 + count + (s + 1) * bits] for s in range(count)]
    shot_dev, det_dev = raw.shape
    block_rows = PB // shot_count
    groups = shot_count // 2
    me = lax.axis_index("shot")
    my_det = lax.axis_index("det")
    shot_total = float(shot_dev * shot_count)
    inverse = 1.0 / shot_total
    bit = [(me // (1 << b)) % 2 for b in range(bits)]
    partner = [me + (1 - 2 * bit[b]) * (1 << b) for b in range(bits)]
    mesh_id = pl.DeviceIdType.MESH

    chunk = shot_dev // load_chunks
    copies = []
    for c in range(load_chunks):
        copy = pltpu.make_async_copy(
            events_ref.at[pl.ds(c * chunk, chunk), :], raw.at[pl.ds(c * chunk, chunk), :], in_sem.at[c])
        copy.start()
        copies.append(copy)
    barrier = pltpu.get_barrier_semaphore()
    for b in range(2):
        pl.semaphore_signal(barrier, inc=1, device_id={"shot": partner[b]}, device_id_type=mesh_id)
    has_up, has_down = me + 4 < shot_count, me >= 4

    def signal_line(sem):
        @pl.when(has_up)
        def _():
            pl.semaphore_signal(sem, inc=1, device_id={"shot": me + 4}, device_id_type=mesh_id)

        @pl.when(has_down)
        def _():
            pl.semaphore_signal(sem, inc=1, device_id={"shot": me - 4}, device_id_type=mesh_id)

    signal_line(barrier)
    line_count = has_up.astype(jnp.int32) + has_down.astype(jnp.int32)
    for d in range(1, det_count):
        pl.semaphore_signal(barrier, inc=1, device_id={"det": (my_det + d) % det_count}, device_id_type=mesh_id)

    def make_slot_table():
        lanes = 128
        lane = lax.broadcasted_iota(jnp.int32, (shot_count, lanes), 1)
        owner = lax.broadcasted_iota(jnp.int32, (shot_count, lanes), 0)
        hit_first = (tables_ref[2, :, 0:lanes] == owner).astype(jnp.int32)
        hit_second = (tables_ref[3, :, 0:lanes] == owner).astype(jnp.int32)
        both = hit_first + hit_second
        upto = both
        shift = 1
        while shift < pair_count:
            upto = upto + jnp.where(lane >= shift, pltpu.roll(upto, shift, 1), 0)
            shift *= 2
        rank_first = upto - both
        rank_second = rank_first + hit_first
        table = jnp.zeros((shot_count, lanes), jnp.int32)
        for j in range(recv_slots):
            pick = (jnp.where(rank_first == j, hit_first, 0) + jnp.where(rank_second == j, hit_second, 0))
            index = pair_count + jnp.sum(pick * (lane - pair_count), axis=1, keepdims=True)
            table = jnp.where(lane == j, index, table)
        slot_vector[...] = table
        copy = pltpu.make_async_copy(slot_vector, slot_table, table_sem)
        copy.start()
        return copy

    for c in range(load_chunks):
        copies[c].wait()
        piece = raw[pl.ds(c * chunk, chunk), :].astype(jnp.float32).astype(jnp.bfloat16)
        turned[:, :, pl.ds(c * chunk, chunk)] = piece.T.reshape(patch_dev, PB, chunk)

    nt = (((1,), (1,)), ((), ()))

    def stream_base(s, t):
        dims = streams[s][2]
        base = 0
        for i in range(t):
            base = base + bit[dims[i]] * (1 << (len(dims) - 1 - i))
        return base

    def stream_copy(s, t):
        dims = streams[s][2]
        if t == len(dims):
            source = held[s].at[pl.ds(stream_base(s, t), 1)]
            other = partner[bits - 1]
        else:
            length = 1 << (len(dims) - 1 - t)
            source = held[s].at[pl.ds(stream_base(s, t) + (1 - bit[dims[t]]) * length, length)]
            other = partner[dims[t]]
        return pltpu.make_async_remote_copy(
            src_ref=source, dst_ref=landed[s][t], send_sem=send_sem.at[s, t], recv_sem=recv_sem.at[s, t],
            device_id={"shot": other}, device_id_type=mesh_id)

    def place(dims, g):
        return sum(((g >> dims[i]) & 1) << (len(dims) - 1 - i) for i in range(len(dims)))

    owner_of = {}
    for s, (kind, tile, _, start, size) in enumerate(streams):
        for k in range(size):
            owner_of[kind, tile, start + k] = (s, k)
    done = set()

    def put(s):
        kind, _, _, start, size = streams[s]
        for k in range(start, start + size):
            if (kind, k) in done:
                continue
            done.add((kind, k))
            if kind == "intra":
                left, right = turned[k], turned[k]
            else:
                left, right = turned[ends_ref[0, 0, k]], turned[ends_ref[1, 0, k]]
            gram = lax.dot_general(left, right, nt, preferred_element_type=jnp.float32)
            if kind == "intra":
                where = [(0, g, g) for g in range(shot_count)]
            else:
                where = [(i, g, i * groups + g) for i in range(tiles) for g in range(groups)]
            for i, g, row in where:
                to, at = owner_of[kind, i, k]
                held[to][place(streams[to][2], g), at] = gram[row * block_rows:(row + 1) * block_rows]

    lead = []
    for op in ORDER:
        if op[0] != "start":
            break
        lead.append(op[1])
    waits = ["relay"]

    def send(s, t):
        dims = streams[s][2]
        if waits and (t == len(dims) or dims[t] == bits - 1):
            waits.clear()
            pl.semaphore_wait(relay, line_count)
        stream_copy(s, t).start()

    for n, s in enumerate(lead):
        put(s)
        if n == 0:
            pl.semaphore_wait(barrier, 2 + line_count + det_count - 1)
            signal_line(relay)
        send(s, 0)
    for s in range(count):
        put(s)

    def triple_counts(c):
        column = lax.broadcasted_iota(jnp.int32, (128, det_dev), 1)
        lane = lax.broadcasted_iota(jnp.int32, (128, 128), 1)
        bit_rows = []
        for m in range(3):
            named = jnp.broadcast_to(tables_ref[4 + m, :, pl.ds(c * 128, 128)], (128, 128)).T[:, 0:1]
            bit_rows.append(
                jnp.dot((named == column).astype(jnp.float32).astype(jnp.bfloat16),
                        turned[...].reshape(det_dev, shot_dev), preferred_element_type=jnp.float32))
        one, two, three = bit_rows
        both = one * two
        terms = [one, two, three, both, one * three, two * three, both * three]
        packed = jnp.zeros((128, 128), jnp.float32)
        for q, term in enumerate(terms):
            packed = jnp.where(lane == q, jnp.sum(term, axis=1, keepdims=True), packed)
        aux[0, pl.ds(patch_dev + 8 * c, 8), :] = packed.T[0:8]

    def aux_copy(t):
        return pltpu.make_async_remote_copy(
            src_ref=aux.at[t], dst_ref=aux_in.at[t], send_sem=aux_send.at[t], recv_sem=aux_recv.at[t],
            device_id={"shot": partner[t]}, device_id_type=mesh_id)

    pending = []

    def send_aux():
        ones = jnp.ones((8, shot_dev), jnp.bfloat16)
        for p in range(patch_dev):
            total = lax.dot_general(ones, turned[p], nt, preferred_element_type=jnp.float32)
            aux[0, pl.ds(p, 1), :] = total[0:1]
        aux_copy(0).start()
        pending.append(make_slot_table())

    unfitted = []
    means = []

    def fit_pairs():
        while means and unfitted:
            _, i, _, start, size = streams[unfitted.pop()]
            for k in range(start, start + size):
                fitted[i, k] = rates(pair_sum[i, k], row_buf[i, ends_ref[0, 0, k]], col_buf[ends_ref[1, 0, k]])

    def step(s, t):
        kind, tile, dims, start, size = streams[s]
        depth = len(dims)
        stream_copy(s, t).wait_recv()
        base = stream_base(s, min(t + 1, depth))
        if t == depth:
            pair_sum[tile, pl.ds(start, size)] = held[s][base] + landed[s][t][0]
            unfitted.append(s)
            fit_pairs()
        elif t == depth - 1 and kind == "intra":
            intra_sum[pl.ds(start, size)] = held[s][base] + landed[s][t][0]
        elif t == depth - 1:
            held[s][base] = held[s][base] + landed[s][t][0]
            send(s, t + 1)
        else:
            half = 1 << (depth - 2 - t)
            away = (1 - bit[dims[t + 1]]) * half
            keep = bit[dims[t + 1]] * half

            def add(part):
                mine = pl.ds(base + part, half)
                held[s][mine] = held[s][mine] + landed[s][t][pl.ds(part, half)]
            add(away)
            send(s, t + 1)
            add(keep)

    def rates(coincide, row_rate, col_rate):
        joint_rate = coincide * inverse
        denominator = jnp.maximum(1.0 - 2.0 * row_rate - 2.0 * col_rate + 4.0 * joint_rate, 0.25)
        excess = (joint_rate - row_rate * col_rate) / denominator
        return 100.0 * (0.5 - 0.5 * jnp.sqrt(jnp.maximum(1.0 - 4.0 * excess, 0.04)))

    my_group = me % groups

    def tile_row(i):
        return pl.multiple_of((i * groups + my_group) * block_rows, block_rows)

    def make_means():
        rows = aux[bits]
        turned_counts[...] = jnp.concatenate(
            [rows * inverse, jnp.zeros((PB - rows.shape[0], PB), jnp.float32)], axis=0).T
        starts = [tile_row(i) for i in range(tiles)] + [pl.multiple_of(me * block_rows, block_rows)]
        for i, row in enumerate(starts):
            piece = turned_counts[pl.ds(row, block_rows), :]
            for p in range(patch_dev):
                row_buf[i, p] = jnp.broadcast_to(piece[:, p:p + 1], (block_rows, PB))
        for p in range(patch_dev):
            col_buf[p] = jnp.broadcast_to(aux[bits, pl.ds(p, 1), :] * inverse, (block_rows, PB))
        fitted[:, pair_count] = jnp.zeros((tiles, block_rows, PB), jnp.float32)
        for c in range(triple_count // 128):
            sums = aux[bits, pl.ds(patch_dev + 8 * c, 8), :] * inverse
            first, second, third = sums[0:1], sums[1:2], sums[2:3]
            kappa = (sums[6:7] - sums[3:4] * third - sums[4:5] * second - sums[5:6] * first
                     + 2.0 * first * second * third)
            row = (patch_dev + det_count) * block_rows + c
            packed_ref[recv_slots, row:row + 1, :] = 1000.0 * kappa

    def out_copy(i, m):
        other = me
        for b in range(bits - 1):
            if (m >> b) & 1:
                other = other + (1 - 2 * bit[b]) * (1 << b)
        return other, pltpu.make_async_remote_copy(
            src_ref=outgoing.at[i, m], dst_ref=packed_ref.at[pl.ds(0, recv_slots), pl.ds(tile_row(i), block_rows), :],
            send_sem=out_send.at[i, m], recv_sem=out_recv.at[i, m],
            device_id={"shot": other}, device_id_type=mesh_id)

    def route(i):
        if pending:
            pending.pop().wait()

        for m in reversed(range(1, groups)):
            other, copy = out_copy(i, m)
            for j in range(recv_slots):
                outgoing[i, m, j] = fitted[i, slot_table[other, j]]
            copy.start()
        for j in range(recv_slots):
            packed_ref[j, pl.ds(tile_row(i), block_rows), :] = fitted[i, slot_table[me, j]]

    load_rows = pl.ds(pl.multiple_of((patch_dev + my_det) * block_rows, block_rows), block_rows)

    def load_copy(d):
        return pltpu.make_async_remote_copy(
            src_ref=load_mine, dst_ref=packed_ref.at[recv_slots, load_rows, :], send_sem=load_send.at[d], recv_sem=load_recv.at[d],
            device_id={"det": (my_det + d) % det_count}, device_id_type=mesh_id)

    def finish_intra():
        col = lax.broadcasted_iota(jnp.int32, (block_rows, PB), 1)
        loads = jnp.zeros((block_rows, PB), jnp.float32)
        for p in range(patch_dev):
            fit = rates(intra_sum[p], row_buf[tiles, p], col_buf[p])
            packed_ref[recv_slots, p * block_rows:(p + 1) * block_rows, :] = fit
            loads = jnp.where(col == my_det * patch_dev + p, jnp.sum(fit, axis=1, keepdims=True), loads)
        load_mine[...] = loads
        for d in range(1, det_count):
            load_copy(d).start()
        packed_ref[recv_slots, load_rows, :] = loads

    for op in ORDER[len(lead):]:
        if op[0] == "start":
            send(op[1], 0)
        elif op[0] == "triples":
            for c in range(op[1], triple_count // 128, 2):
                triple_counts(c)
        elif op[0] == "counts":
            send_aux()
        elif op[0] == "aux":
            t = op[1]
            aux_copy(t).wait_recv()
            aux[t + 1] = aux[t] + aux_in[t]
            if t == bits - 1:
                make_means()
                means.append(True)
                fit_pairs()
            else:
                if t == bits - 2 and waits:
                    waits.clear()
                    pl.semaphore_wait(relay, line_count)
                aux_copy(t + 1).start()
        elif op[0] == "route":
            route(op[1])
        elif op[0] == "intra":
            finish_intra()
        else:
            step(*op)

    for d in range(1, det_count):
        load_copy(d).wait()
    for i in range(tiles):
        for m in range(1, groups):
            out_copy(i, m)[1].wait()
    for t in range(bits):
        aux_copy(t).wait_send()
        for s in range(count):
            stream_copy(s, t).wait_send()


def local_fused(events, pair_patches, pair_owners, triples, det_count):
    shot_dev, det_dev = events.shape
    shot_count = lax.axis_size("shot")
    bits = shot_count.bit_length() - 1
    patch_dev = det_dev // PB
    block_rows = PB // shot_count
    pair_count = pair_patches.shape[1]
    triple_count = triples.shape[1]
    recv_slots = max(2, 4 * pair_count // shot_count)
    streams = plan_streams(patch_dev, pair_count)
    load_chunks = 4
    tiles = 2
    smem = pl.BlockSpec(memory_space=pltpu.SMEM)
    vmem = pl.BlockSpec(memory_space=pltpu.VMEM)
    plan = (streams, shot_count, det_count, patch_dev, pair_count, triple_count, recv_slots, load_chunks, tiles)
    aux_rows = patch_dev + 8 * (triple_count // 128)
    f32 = jnp.float32
    dma = pltpu.SemaphoreType.DMA
    count = len(streams)
    tile = (block_rows, PB)
    scratch = [
        pltpu.VMEM((shot_dev, det_dev), jnp.int32),
        pltpu.VMEM((patch_dev, PB, shot_dev), jnp.bfloat16),
        pltpu.VMEM((bits + 1, aux_rows, 128), f32),
        pltpu.VMEM((bits, aux_rows, 128), f32),
        pltpu.VMEM((patch_dev, *tile), f32),
        pltpu.VMEM((tiles, pair_count, *tile), f32),
        pltpu.VMEM((PB, PB), f32),
        pltpu.VMEM((tiles + 1, patch_dev, *tile), f32),
        pltpu.VMEM((patch_dev, *tile), f32),
        pltpu.VMEM((tiles, pair_count + 1, *tile), f32),
        pltpu.VMEM((tiles, shot_count // 2, recv_slots, *tile), f32),
        pltpu.VMEM(tile, f32),
        pltpu.VMEM((shot_count, 128), jnp.int32),
        pltpu.SMEM((shot_count, 128), jnp.int32),
        dma((load_chunks,)), dma((count, bits)), dma((count, bits)), dma((bits,)), dma((bits,)),
        dma((tiles, shot_count // 2)), dma((tiles, shot_count // 2)), dma((det_count,)), dma((det_count,)),
        pltpu.SemaphoreType.REGULAR, dma,
    ]
    scratch += [pltpu.VMEM((1 << len(dims), size, *tile), f32) for _, _, dims, _, size in streams]
    for _, _, dims, _, size in streams:
        scratch += [pltpu.VMEM((max(1, (1 << len(dims)) >> (t + 1)), size, *tile), f32) for t in range(bits)]
    def lanes(rows, fill):
        rows = jnp.transpose(rows, (2, 0, 1))
        return jnp.pad(rows, ((0, 0), (0, 0), (0, triple_count - pair_count)), constant_values=fill)

    tables = jnp.concatenate(
        [lanes(pair_patches, 0), lanes(pair_owners, -1), jnp.transpose(triples, (2, 0, 1))], axis=0)
    packed = pl.pallas_call(
        functools.partial(fused_kernel, plan),
        out_shape=jax.ShapeDtypeStruct((recv_slots + 1, PB, PB), f32),
        in_specs=[pl.BlockSpec(memory_space=pltpu.HBM), smem, vmem],
        out_specs=vmem,
        scratch_shapes=scratch,
        compiler_params=pltpu.CompilerParams(
            collective_id=0, has_side_effects=True, vmem_limit_bytes=VMEM_BYTES),
    )(events, tables, tables)
    hbm = pl.BlockSpec(memory_space=pltpu.HBM)
    intra, boundary, load, kappa = pl.pallas_call(
        functools.partial(finish_kernel, patch_dev, det_count),
        out_shape=(
            jax.ShapeDtypeStruct((patch_dev * block_rows, PB), f32),
            jax.ShapeDtypeStruct((recv_slots, PB, PB), f32),
            jax.ShapeDtypeStruct((block_rows, det_count * patch_dev), f32),
            jax.ShapeDtypeStruct((1, triple_count), f32),
        ),
        in_specs=[vmem],
        out_specs=(hbm, hbm, vmem, vmem),
        scratch_shapes=[dma((2,))],
        compiler_params=pltpu.CompilerParams(vmem_limit_bytes=4 * 1024 * 1024),
    )(packed)
    return (intra.reshape(patch_dev, block_rows, PB), boundary[None, None], jnp.swapaxes(load, 0, 1), kappa)


def local(events, pair_patches, pair_owners, triples):
    shot_dev, det_dev = events.shape
    shot_count = lax.axis_size("shot")
    shot_index = lax.axis_index("shot")
    shot_total = float(shot_dev * shot_count)
    inverse = 1.0 / shot_total
    patch_dev = det_dev // PB
    rows_own = PB // shot_count
    pair_count = pair_patches.shape[1]
    triple_count = triples.shape[1]
    recv_slots = max(2, 4 * pair_count // shot_count)
    bit_matrix = events.astype(jnp.bfloat16)
    patches = bit_matrix.reshape(shot_dev, patch_dev, PB)
    local_counts = jnp.sum(events, axis=0).astype(jnp.float32)
    triple_index = triples[0]
    picked = (
        jnp.take(events, triple_index.reshape(-1), axis=1)
        .astype(jnp.float32)
        .reshape(shot_dev, triple_count, 3)
    )
    first_bit = picked[:, :, 0]
    second_bit = picked[:, :, 1]
    third_bit = picked[:, :, 2]
    triple_terms = jnp.stack(
        [
            jnp.sum(first_bit * second_bit, axis=0),
            jnp.sum(first_bit * third_bit, axis=0),
            jnp.sum(second_bit * third_bit, axis=0),
            jnp.sum(first_bit * second_bit * third_bit, axis=0),
        ]
    )
    intra = jnp.einsum("sai,saj->aij", patches, patches, preferred_element_type=jnp.float32)
    pair_ends = pair_patches[0]

    def pair_gram(ends):
        first = lax.dynamic_slice_in_dim(bit_matrix, ends[0] * PB, PB, 1)
        second = lax.dynamic_slice_in_dim(bit_matrix, ends[1] * PB, PB, 1)
        return lax.dot_general(first, second, (((0,), (0,)), ((), ())), preferred_element_type=jnp.float32)

    cross = lax.map(pair_gram, pair_ends)
    joined = lax.psum_scatter(
        jnp.concatenate([intra, cross], axis=0), "shot", scatter_dimension=1, tiled=True
    )
    intra_share = joined[:patch_dev]
    pair_share = joined[patch_dev:]
    counts, triple_total = lax.psum((local_counts, triple_terms), "shot")
    patch_counts = counts.reshape(patch_dev, PB)
    row_counts = lax.dynamic_slice_in_dim(patch_counts, shot_index * rows_own, rows_own, 1)
    intra_rates = fit_rates(intra_share, row_counts, patch_counts, shot_total)
    load_share = jnp.sum(intra_rates, axis=2)
    detector_load = lax.all_gather(load_share, "det", axis=0, tiled=True)
    pair_slot, valid = route_table(pair_owners[0].reshape(-1), shot_count, recv_slots)
    mine = lax.dynamic_index_in_dim(pair_slot, shot_index, 0, keepdims=False)
    valid_mine = lax.dynamic_index_in_dim(valid, shot_index, 0, keepdims=False)
    fitted = fit_rates(
        pair_share,
        jnp.take(row_counts, pair_ends[:, 0], axis=0),
        jnp.take(patch_counts, pair_ends[:, 1], axis=0),
        shot_total,
    )
    every_block = lax.all_gather(fitted, "shot", axis=1, tiled=True)
    boundary = lax.map(lambda k: lax.dynamic_index_in_dim(every_block, k, 0, keepdims=False), mine)
    boundary = boundary * valid_mine[:, None, None]
    moments = triple_total * inverse
    means = jnp.take(counts, triple_index.reshape(-1), axis=0).reshape(triple_count, 3) * inverse
    mean_first = means[:, 0]
    mean_second = means[:, 1]
    mean_third = means[:, 2]
    kappa = (
        moments[3]
        - moments[0] * mean_third
        - moments[1] * mean_second
        - moments[2] * mean_first
        + 2.0 * mean_first * mean_second * mean_third
    )
    triple_cumulant = 1000.0 * kappa
    return (intra_rates, boundary[None, None], detector_load, triple_cumulant[None])


def solution(mesh):
    placed = (P("shot", "det"), P("det", None, None), P("det", None, None), P("det", None, None))
    shot_count = mesh.shape["shot"]
    det_count = mesh.shape["det"]
    power_of_two = shot_count & (shot_count - 1) == 0 and shot_count > 1
    whole_tiles = PB % shot_count == 0 and (PB // shot_count) % 8 == 0

    def body(events, pair_patches, pair_owners, triples):
        if power_of_two and whole_tiles and shot_count > 8 and triples.shape[1] % 128 == 0:
            return local_fused(events, pair_patches, pair_owners, triples, det_count)
        return local(events, pair_patches, pair_owners, triples)

    return jax.shard_map(
        body,
        mesh=mesh,
        in_specs=placed,
        out_specs=(
            P("det", "shot", None),
            P("det", "shot", None, None, None),
            P(None, "shot"),
            P("det", None),
        ),
        check_vma=False,
    )
```

```python
import functools

import jax
import jax.numpy as jnp
from jax import lax
from jax.experimental import pallas as pl
from jax.experimental.pallas import tpu as pltpu
from jax.sharding import PartitionSpec as P

PB = 128
VMEM_BYTES = 52 * 1024 * 1024


def fit_rates(coincide, row_count, col_count, shot_total):
    inverse = 1.0 / shot_total
    joint_rate = coincide * inverse
    row_rate = row_count[..., :, None] * inverse
    col_rate = col_count[..., None, :] * inverse
    denominator = jnp.maximum(1.0 - 2.0 * row_rate - 2.0 * col_rate + 4.0 * joint_rate, 0.25)
    excess = (joint_rate - row_rate * col_rate) / denominator
    return 100.0 * (0.5 - 0.5 * jnp.sqrt(jnp.maximum(1.0 - 4.0 * excess, 0.04)))


def route_table(owner_row, shot_count, recv_slots):
    owner_ids = jnp.arange(shot_count, dtype=jnp.int32)
    hit = owner_row[None, :] == owner_ids[:, None]
    entry_ids = jnp.arange(owner_row.shape[0], dtype=jnp.int32)
    upto = entry_ids[:, None] >= entry_ids[None, :]
    rank = jnp.sum(jnp.where(hit[:, None, :] & upto[None, :, :], 1, 0), axis=2) - 1
    slot_ids = jnp.arange(recv_slots, dtype=jnp.int32)
    chosen = hit[:, None, :] & (rank[:, None, :] == slot_ids[None, :, None])
    entry_pair = jnp.arange(owner_row.shape[0], dtype=jnp.int32) // 2
    pair_slot = jnp.sum(jnp.where(chosen, entry_pair[None, None, :], 0), axis=2)
    valid = jnp.any(chosen, axis=2).astype(jnp.float32)
    return (pair_slot, valid)


STREAMS = [
    ('pair', 0, (2, 1, 0), 7), ('pair', 0, (1, 0, 2), 5), ('pair', 0, (1, 0, 2), 7), ('pair', 0, (0, 2, 1), 7),
    ('pair', 1, (0, 1, 2), 5), ('pair', 1, (2, 0, 1), 13), ('pair', 1, (0, 2, 1), 8), ('intra', 0, (1, 2, 0, 3), 3),
    ('intra', 0, (1, 0, 2, 3), 5),
]
ORDER = [
    ('start', 4), ('start', 0), ('start', 1), ('start', 3), ('start', 2), ('start', 5), ('start', 6), ('triples', 0),
    (4, 0), (1, 0), (0, 0), ('triples', 1), ('start', 8), (3, 0), ('counts',), (2, 0), (4, 1), (6, 0), (0, 1), (5, 0),
    ('aux', 0), (1, 1), (3, 1), ('start', 7), (4, 2), (2, 1), (0, 2), ('aux', 1), (1, 2), (3, 2), (6, 1), (8, 0),
    (2, 2), (5, 1), (7, 0), ('aux', 2), (6, 2), (8, 1), (1, 3), (5, 2), (7, 1), (3, 3), ('aux', 3), (2, 3), (0, 3),
    ('route', 0), (8, 2), (4, 3), (7, 2), (6, 3), (5, 3), ('route', 1), (8, 3), (7, 3), ('intra',),
]


def plan_streams(patch_dev, pair_count):
    streams = [None] * len(STREAMS)
    for kind in (("pair", 0), ("pair", 1), ("intra", 0)):
        total = pair_count if kind[0] == "pair" else patch_dev
        members = [s for s, stream in enumerate(STREAMS) if stream[:2] == kind]
        whole = sum(STREAMS[s][3] for s in members)
        start, seen = 0, 0
        for s in members:
            seen += STREAMS[s][3]
            stop = total * seen // whole
            streams[s] = (*STREAMS[s][:3], start, stop - start)
            start = stop
    return streams


def finish_kernel(patch_dev, det_count, packed_in, intra_out, boundary_out, load_out, kappa_out,
                  load_buf, kappa_buf, out_sem):
    slots = boundary_out.shape[0]
    rows = intra_out.shape[0]
    parts = 3
    leave = []
    for i in range(parts):
        part = pl.ds(slots * i // parts, slots * (i + 1) // parts - slots * i // parts)
        leave.append(pltpu.make_async_copy(packed_in.at[part], boundary_out.at[part], out_sem.at[i]))
    leave.append(pltpu.make_async_copy(packed_in.at[slots, pl.ds(0, rows)], intra_out, out_sem.at[parts]))
    for copy in leave:
        copy.start()
    height = rows // patch_dev
    total = packed_in[slots, rows:rows + height]
    for d in range(1, det_count):
        total = total + packed_in[slots, rows + d * height:rows + (d + 1) * height]
    load_buf[...] = total[:, 0:load_out.shape[1]]
    first = rows + det_count * height
    for c in range(kappa_out.shape[1] // PB):
        kappa_buf[:, pl.ds(c * PB, PB)] = packed_in[slots, first + c:first + c + 1]
    small = [pltpu.make_async_copy(load_buf, load_out, out_sem.at[parts + 1]),
             pltpu.make_async_copy(kappa_buf, kappa_out, out_sem.at[parts + 2])]
    for copy in small:
        copy.start()
    for copy in leave + small:
        copy.wait()


def fused_kernel(plan, events_ref, ends_ref, tables_ref, packed_ref, *scratch):
    (streams, shot_count, det_count, patch_dev, pair_count, triple_count, recv_slots, load_chunks, tiles) = plan
    bits = shot_count.bit_length() - 1
    count = len(streams)
    raw, turned, aux, aux_in, intra_sum, pair_sum, turned_counts, row_buf, col_buf, fitted, outgoing, load_mine = scratch[:12]
    slot_vector, slot_table = scratch[12:14]
    (in_sem, send_sem, recv_sem, aux_send, aux_recv, out_send, out_recv, load_send, load_recv, relay,
     table_sem) = scratch[14:25]
    held = scratch[25:25 + count]
    landed = [scratch[25 + count + s * bits:25 + count + (s + 1) * bits] for s in range(count)]
    shot_dev, det_dev = raw.shape
    block_rows = PB // shot_count
    groups = shot_count // 2
    me = lax.axis_index("shot")
    my_det = lax.axis_index("det")
    shot_total = float(shot_dev * shot_count)
    inverse = 1.0 / shot_total
    bit = [(me // (1 << b)) % 2 for b in range(bits)]
    partner = [me + (1 - 2 * bit[b]) * (1 << b) for b in range(bits)]
    mesh_id = pl.DeviceIdType.MESH

    chunk = shot_dev // load_chunks
    copies = []
    for c in range(load_chunks):
        copy = pltpu.make_async_copy(
            events_ref.at[pl.ds(c * chunk, chunk), :], raw.at[pl.ds(c * chunk, chunk), :], in_sem.at[c])
        copy.start()
        copies.append(copy)
    barrier = pltpu.get_barrier_semaphore()
    for b in range(2):
        pl.semaphore_signal(barrier, inc=1, device_id={"shot": partner[b]}, device_id_type=mesh_id)
    has_up, has_down = me + 4 < shot_count, me >= 4

    def signal_line(sem):
        @pl.when(has_up)
        def _():
            pl.semaphore_signal(sem, inc=1, device_id={"shot": me + 4}, device_id_type=mesh_id)

        @pl.when(has_down)
        def _():
            pl.semaphore_signal(sem, inc=1, device_id={"shot": me - 4}, device_id_type=mesh_id)

    signal_line(barrier)
    line_count = has_up.astype(jnp.int32) + has_down.astype(jnp.int32)
    for d in range(1, det_count):
        pl.semaphore_signal(barrier, inc=1, device_id={"det": (my_det + d) % det_count}, device_id_type=mesh_id)

    def make_slot_table():
        lanes = 128
        lane = lax.broadcasted_iota(jnp.int32, (shot_count, lanes), 1)
        owner = lax.broadcasted_iota(jnp.int32, (shot_count, lanes), 0)
        hit_first = (tables_ref[2, :, 0:lanes] == owner).astype(jnp.int32)
        hit_second = (tables_ref[3, :, 0:lanes] == owner).astype(jnp.int32)
        both = hit_first + hit_second
        upto = both
        shift = 1
        while shift < pair_count:
            upto = upto + jnp.where(lane >= shift, pltpu.roll(upto, shift, 1), 0)
            shift *= 2
        rank_first = upto - both
        rank_second = rank_first + hit_first
        table = jnp.zeros((shot_count, lanes), jnp.int32)
        for j in range(recv_slots):
            pick = (jnp.where(rank_first == j, hit_first, 0) + jnp.where(rank_second == j, hit_second, 0))
            index = pair_count + jnp.sum(pick * (lane - pair_count), axis=1, keepdims=True)
            table = jnp.where(lane == j, index, table)
        slot_vector[...] = table
        copy = pltpu.make_async_copy(slot_vector, slot_table, table_sem)
        copy.start()
        return copy

    for c in range(load_chunks):
        copies[c].wait()
        piece = raw[pl.ds(c * chunk, chunk), :].astype(jnp.float32).T
        turned[:, :, pl.ds(c * chunk, chunk)] = piece.astype(jnp.bfloat16).reshape(patch_dev, PB, chunk)

    nt = (((1,), (1,)), ((), ()))

    def stream_base(s, t):
        dims = streams[s][2]
        base = 0
        for i in range(t):
            base = base + bit[dims[i]] * (1 << (len(dims) - 1 - i))
        return base

    def stream_copy(s, t):
        dims = streams[s][2]
        if t == len(dims):
            source = held[s].at[pl.ds(stream_base(s, t), 1)]
            other = partner[bits - 1]
        else:
            length = 1 << (len(dims) - 1 - t)
            source = held[s].at[pl.ds(stream_base(s, t) + (1 - bit[dims[t]]) * length, length)]
            other = partner[dims[t]]
        return pltpu.make_async_remote_copy(
            src_ref=source, dst_ref=landed[s][t], send_sem=send_sem.at[s, t], recv_sem=recv_sem.at[s, t],
            device_id={"shot": other}, device_id_type=mesh_id)

    def place(dims, g):
        return sum(((g >> dims[i]) & 1) << (len(dims) - 1 - i) for i in range(len(dims)))

    owner_of = {}
    for s, (kind, tile, _, start, size) in enumerate(streams):
        for k in range(size):
            owner_of[kind, tile, start + k] = (s, k)
    done = set()

    def put(s):
        kind, _, _, start, size = streams[s]
        for k in range(start, start + size):
            if (kind, k) in done:
                continue
            done.add((kind, k))
            if kind == "intra":
                left, right = turned[k], turned[k]
            else:
                left, right = turned[ends_ref[0, 0, k]], turned[ends_ref[1, 0, k]]
            gram = lax.dot_general(left, right, nt, preferred_element_type=jnp.float32)
            if kind == "intra":
                where = [(0, g, g) for g in range(shot_count)]
            else:
                where = [(i, g, i * groups + g) for i in range(tiles) for g in range(groups)]
            for i, g, row in where:
                to, at = owner_of[kind, i, k]
                held[to][place(streams[to][2], g), at] = gram[row * block_rows:(row + 1) * block_rows]

    lead = []
    for op in ORDER:
        if op[0] != "start":
            break
        lead.append(op[1])
    waits = ["relay"]

    def send(s, t):
        dims = streams[s][2]
        if waits and (t == len(dims) or dims[t] == bits - 1):
            waits.clear()
            pl.semaphore_wait(relay, line_count)
        stream_copy(s, t).start()

    for n, s in enumerate(lead):
        put(s)
        if n == 0:
            pl.semaphore_wait(barrier, 2 + line_count + det_count - 1)
            signal_line(relay)
        send(s, 0)
    for s in range(count):
        put(s)

    def triple_counts(c):
        column = lax.broadcasted_iota(jnp.int32, (128, det_dev), 1)
        lane = lax.broadcasted_iota(jnp.int32, (128, 128), 1)
        bit_rows = []
        for m in range(3):
            named = jnp.broadcast_to(tables_ref[4 + m, :, pl.ds(c * 128, 128)], (128, 128)).T[:, 0:1]
            bit_rows.append(
                jnp.dot((named == column).astype(jnp.float32).astype(jnp.bfloat16),
                        turned[...].reshape(det_dev, shot_dev), preferred_element_type=jnp.float32))
        one, two, three = bit_rows
        both = one * two
        terms = [one, two, three, both, one * three, two * three, both * three]
        packed = jnp.zeros((128, 128), jnp.float32)
        for q, term in enumerate(terms):
            packed = jnp.where(lane == q, jnp.sum(term, axis=1, keepdims=True), packed)
        aux[0, pl.ds(patch_dev + 8 * c, 8), :] = packed.T[0:8]

    def aux_copy(t):
        return pltpu.make_async_remote_copy(
            src_ref=aux.at[t], dst_ref=aux_in.at[t], send_sem=aux_send.at[t], recv_sem=aux_recv.at[t],
            device_id={"shot": partner[t]}, device_id_type=mesh_id)

    pending = []

    def send_aux():
        ones = jnp.ones((8, shot_dev), jnp.bfloat16)
        for p in range(patch_dev):
            total = lax.dot_general(ones, turned[p], nt, preferred_element_type=jnp.float32)
            aux[0, pl.ds(p, 1), :] = total[0:1]
        aux_copy(0).start()
        pending.append(make_slot_table())

    unfitted = []
    means = []

    def fit_pairs():
        while means and unfitted:
            _, i, _, start, size = streams[unfitted.pop()]
            for k in range(start, start + size):
                fitted[i, k] = rates(pair_sum[i, k], row_buf[i, ends_ref[0, 0, k]], col_buf[ends_ref[1, 0, k]])

    def step(s, t):
        kind, tile, dims, start, size = streams[s]
        depth = len(dims)
        stream_copy(s, t).wait_recv()
        base = stream_base(s, min(t + 1, depth))
        if t == depth:
            pair_sum[tile, pl.ds(start, size)] = held[s][base] + landed[s][t][0]
            unfitted.append(s)
            fit_pairs()
        elif t == depth - 1 and kind == "intra":
            intra_sum[pl.ds(start, size)] = held[s][base] + landed[s][t][0]
        elif t == depth - 1:
            held[s][base] = held[s][base] + landed[s][t][0]
            send(s, t + 1)
        else:
            half = 1 << (depth - 2 - t)
            away = (1 - bit[dims[t + 1]]) * half
            keep = bit[dims[t + 1]] * half

            def add(part):
                mine = pl.ds(base + part, half)
                held[s][mine] = held[s][mine] + landed[s][t][pl.ds(part, half)]
            add(away)
            send(s, t + 1)
            add(keep)

    def rates(coincide, row_rate, col_rate):
        joint_rate = coincide * inverse
        denominator = jnp.maximum(1.0 - 2.0 * row_rate - 2.0 * col_rate + 4.0 * joint_rate, 0.25)
        excess = (joint_rate - row_rate * col_rate) / denominator
        return 100.0 * (0.5 - 0.5 * jnp.sqrt(jnp.maximum(1.0 - 4.0 * excess, 0.04)))

    my_group = me % groups

    def tile_row(i):
        return pl.multiple_of((i * groups + my_group) * block_rows, block_rows)

    def make_means():
        rows = aux[bits]
        turned_counts[...] = jnp.concatenate(
            [rows * inverse, jnp.zeros((PB - rows.shape[0], PB), jnp.float32)], axis=0).T
        starts = [tile_row(i) for i in range(tiles)] + [pl.multiple_of(me * block_rows, block_rows)]
        for i, row in enumerate(starts):
            piece = turned_counts[pl.ds(row, block_rows), :]
            for p in range(patch_dev):
                row_buf[i, p] = jnp.broadcast_to(piece[:, p:p + 1], (block_rows, PB))
        for p in range(patch_dev):
            col_buf[p] = jnp.broadcast_to(aux[bits, pl.ds(p, 1), :] * inverse, (block_rows, PB))
        fitted[:, pair_count] = jnp.zeros((tiles, block_rows, PB), jnp.float32)
        for c in range(triple_count // 128):
            sums = aux[bits, pl.ds(patch_dev + 8 * c, 8), :] * inverse
            first, second, third = sums[0:1], sums[1:2], sums[2:3]
            kappa = (sums[6:7] - sums[3:4] * third - sums[4:5] * second - sums[5:6] * first
                     + 2.0 * first * second * third)
            row = (patch_dev + det_count) * block_rows + c
            packed_ref[recv_slots, row:row + 1, :] = 1000.0 * kappa

    def out_copy(i, m):
        other = me
        for b in range(bits - 1):
            if (m >> b) & 1:
                other = other + (1 - 2 * bit[b]) * (1 << b)
        return other, pltpu.make_async_remote_copy(
            src_ref=outgoing.at[i, m], dst_ref=packed_ref.at[pl.ds(0, recv_slots), pl.ds(tile_row(i), block_rows), :],
            send_sem=out_send.at[i, m], recv_sem=out_recv.at[i, m],
            device_id={"shot": other}, device_id_type=mesh_id)

    def route(i):
        if pending:
            pending.pop().wait()

        for m in reversed(range(1, groups)):
            other, copy = out_copy(i, m)
            for j in range(recv_slots):
                outgoing[i, m, j] = fitted[i, slot_table[other, j]]
            copy.start()
        for j in range(recv_slots):
            packed_ref[j, pl.ds(tile_row(i), block_rows), :] = fitted[i, slot_table[me, j]]

    load_rows = pl.ds(pl.multiple_of((patch_dev + my_det) * block_rows, block_rows), block_rows)

    def load_copy(d):
        return pltpu.make_async_remote_copy(
            src_ref=load_mine, dst_ref=packed_ref.at[recv_slots, load_rows, :], send_sem=load_send.at[d], recv_sem=load_recv.at[d],
            device_id={"det": (my_det + d) % det_count}, device_id_type=mesh_id)

    def finish_intra():
        col = lax.broadcasted_iota(jnp.int32, (block_rows, PB), 1)
        loads = jnp.zeros((block_rows, PB), jnp.float32)
        for p in range(patch_dev):
            fit = rates(intra_sum[p], row_buf[tiles, p], col_buf[p])
            packed_ref[recv_slots, p * block_rows:(p + 1) * block_rows, :] = fit
            loads = jnp.where(col == my_det * patch_dev + p, jnp.sum(fit, axis=1, keepdims=True), loads)
        load_mine[...] = loads
        for d in range(1, det_count):
            load_copy(d).start()
        packed_ref[recv_slots, load_rows, :] = loads

    for op in ORDER[len(lead):]:
        if op[0] == "start":
            send(op[1], 0)
        elif op[0] == "triples":
            for c in range(op[1], triple_count // 128, 2):
                triple_counts(c)
        elif op[0] == "counts":
            send_aux()
        elif op[0] == "aux":
            t = op[1]
            aux_copy(t).wait_recv()
            aux[t + 1] = aux[t] + aux_in[t]
            if t == bits - 1:
                make_means()
                means.append(True)
                fit_pairs()
            else:
                if t == bits - 2 and waits:
                    waits.clear()
                    pl.semaphore_wait(relay, line_count)
                aux_copy(t + 1).start()
        elif op[0] == "route":
            route(op[1])
        elif op[0] == "intra":
            finish_intra()
        else:
            step(*op)

    for t in range(bits):
        aux_copy(t).wait_send()
        for s in range(count):
            stream_copy(s, t).wait_send()
    for d in range(1, det_count):
        load_copy(d).wait()
    for i in range(tiles):
        for m in range(1, groups):
            out_copy(i, m)[1].wait()


def local_fused(events, pair_patches, pair_owners, triples, det_count):
    shot_dev, det_dev = events.shape
    shot_count = lax.axis_size("shot")
    bits = shot_count.bit_length() - 1
    patch_dev = det_dev // PB
    block_rows = PB // shot_count
    pair_count = pair_patches.shape[1]
    triple_count = triples.shape[1]
    recv_slots = max(2, 4 * pair_count // shot_count)
    streams = plan_streams(patch_dev, pair_count)
    load_chunks = 4
    tiles = 2
    smem = pl.BlockSpec(memory_space=pltpu.SMEM)
    vmem = pl.BlockSpec(memory_space=pltpu.VMEM)
    plan = (streams, shot_count, det_count, patch_dev, pair_count, triple_count, recv_slots, load_chunks, tiles)
    aux_rows = patch_dev + 8 * (triple_count // 128)
    f32 = jnp.float32
    dma = pltpu.SemaphoreType.DMA
    count = len(streams)
    tile = (block_rows, PB)
    scratch = [
        pltpu.VMEM((shot_dev, det_dev), jnp.int32),
        pltpu.VMEM((patch_dev, PB, shot_dev), jnp.bfloat16),
        pltpu.VMEM((bits + 1, aux_rows, 128), f32),
        pltpu.VMEM((bits, aux_rows, 128), f32),
        pltpu.VMEM((patch_dev, *tile), f32),
        pltpu.VMEM((tiles, pair_count, *tile), f32),
        pltpu.VMEM((PB, PB), f32),
        pltpu.VMEM((tiles + 1, patch_dev, *tile), f32),
        pltpu.VMEM((patch_dev, *tile), f32),
        pltpu.VMEM((tiles, pair_count + 1, *tile), f32),
        pltpu.VMEM((tiles, shot_count // 2, recv_slots, *tile), f32),
        pltpu.VMEM(tile, f32),
        pltpu.VMEM((shot_count, 128), jnp.int32),
        pltpu.SMEM((shot_count, 128), jnp.int32),
        dma((load_chunks,)), dma((count, bits)), dma((count, bits)), dma((bits,)), dma((bits,)),
        dma((tiles, shot_count // 2)), dma((tiles, shot_count // 2)), dma((det_count,)), dma((det_count,)),
        pltpu.SemaphoreType.REGULAR, dma,
    ]
    scratch += [pltpu.VMEM((1 << len(dims), size, *tile), f32) for _, _, dims, _, size in streams]
    for _, _, dims, _, size in streams:
        scratch += [pltpu.VMEM((max(1, (1 << len(dims)) >> (t + 1)), size, *tile), f32) for t in range(bits)]
    def lanes(rows, fill):
        rows = jnp.transpose(rows, (2, 0, 1))
        return jnp.pad(rows, ((0, 0), (0, 0), (0, triple_count - pair_count)), constant_values=fill)

    tables = jnp.concatenate(
        [lanes(pair_patches, 0), lanes(pair_owners, -1), jnp.transpose(triples, (2, 0, 1))], axis=0)
    packed = pl.pallas_call(
        functools.partial(fused_kernel, plan),
        out_shape=jax.ShapeDtypeStruct((recv_slots + 1, PB, PB), f32),
        in_specs=[pl.BlockSpec(memory_space=pltpu.HBM), smem, vmem],
        out_specs=vmem,
        scratch_shapes=scratch,
        compiler_params=pltpu.CompilerParams(
            collective_id=0, has_side_effects=True, vmem_limit_bytes=VMEM_BYTES),
    )(events, tables, tables)
    hbm = pl.BlockSpec(memory_space=pltpu.HBM)
    intra, boundary, load, kappa = pl.pallas_call(
        functools.partial(finish_kernel, patch_dev, det_count),
        out_shape=(
            jax.ShapeDtypeStruct((patch_dev * block_rows, PB), f32),
            jax.ShapeDtypeStruct((recv_slots, PB, PB), f32),
            jax.ShapeDtypeStruct((block_rows, det_count * patch_dev), f32),
            jax.ShapeDtypeStruct((1, triple_count), f32),
        ),
        in_specs=[vmem],
        out_specs=(hbm, hbm, hbm, hbm),
        scratch_shapes=[
            pltpu.VMEM((block_rows, det_count * patch_dev), f32), pltpu.VMEM((1, triple_count), f32), dma((6,))],
        compiler_params=pltpu.CompilerParams(vmem_limit_bytes=4 * 1024 * 1024),
    )(packed)
    return (intra.reshape(patch_dev, block_rows, PB), boundary[None, None], jnp.swapaxes(load, 0, 1), kappa)


def local(events, pair_patches, pair_owners, triples):
    shot_dev, det_dev = events.shape
    shot_count = lax.axis_size("shot")
    shot_index = lax.axis_index("shot")
    shot_total = float(shot_dev * shot_count)
    inverse = 1.0 / shot_total
    patch_dev = det_dev // PB
    rows_own = PB // shot_count
    pair_count = pair_patches.shape[1]
    triple_count = triples.shape[1]
    recv_slots = max(2, 4 * pair_count // shot_count)
    bit_matrix = events.astype(jnp.bfloat16)
    patches = bit_matrix.reshape(shot_dev, patch_dev, PB)
    local_counts = jnp.sum(events, axis=0).astype(jnp.float32)
    triple_index = triples[0]
    picked = (
        jnp.take(events, triple_index.reshape(-1), axis=1)
        .astype(jnp.float32)
        .reshape(shot_dev, triple_count, 3)
    )
    first_bit = picked[:, :, 0]
    second_bit = picked[:, :, 1]
    third_bit = picked[:, :, 2]
    triple_terms = jnp.stack(
        [
            jnp.sum(first_bit * second_bit, axis=0),
            jnp.sum(first_bit * third_bit, axis=0),
            jnp.sum(second_bit * third_bit, axis=0),
            jnp.sum(first_bit * second_bit * third_bit, axis=0),
        ]
    )
    intra = jnp.einsum("sai,saj->aij", patches, patches, preferred_element_type=jnp.float32)
    pair_ends = pair_patches[0]

    def pair_gram(ends):
        first = lax.dynamic_slice_in_dim(bit_matrix, ends[0] * PB, PB, 1)
        second = lax.dynamic_slice_in_dim(bit_matrix, ends[1] * PB, PB, 1)
        return lax.dot_general(first, second, (((0,), (0,)), ((), ())), preferred_element_type=jnp.float32)

    cross = lax.map(pair_gram, pair_ends)
    joined = lax.psum_scatter(
        jnp.concatenate([intra, cross], axis=0), "shot", scatter_dimension=1, tiled=True
    )
    intra_share = joined[:patch_dev]
    pair_share = joined[patch_dev:]
    counts, triple_total = lax.psum((local_counts, triple_terms), "shot")
    patch_counts = counts.reshape(patch_dev, PB)
    row_counts = lax.dynamic_slice_in_dim(patch_counts, shot_index * rows_own, rows_own, 1)
    intra_rates = fit_rates(intra_share, row_counts, patch_counts, shot_total)
    load_share = jnp.sum(intra_rates, axis=2)
    detector_load = lax.all_gather(load_share, "det", axis=0, tiled=True)
    pair_slot, valid = route_table(pair_owners[0].reshape(-1), shot_count, recv_slots)
    mine = lax.dynamic_index_in_dim(pair_slot, shot_index, 0, keepdims=False)
    valid_mine = lax.dynamic_index_in_dim(valid, shot_index, 0, keepdims=False)
    fitted = fit_rates(
        pair_share,
        jnp.take(row_counts, pair_ends[:, 0], axis=0),
        jnp.take(patch_counts, pair_ends[:, 1], axis=0),
        shot_total,
    )
    every_block = lax.all_gather(fitted, "shot", axis=1, tiled=True)
    boundary = lax.map(lambda k: lax.dynamic_index_in_dim(every_block, k, 0, keepdims=False), mine)
    boundary = boundary * valid_mine[:, None, None]
    moments = triple_total * inverse
    means = jnp.take(counts, triple_index.reshape(-1), axis=0).reshape(triple_count, 3) * inverse
    mean_first = means[:, 0]
    mean_second = means[:, 1]
    mean_third = means[:, 2]
    kappa = (
        moments[3]
        - moments[0] * mean_third
        - moments[1] * mean_second
        - moments[2] * mean_first
        + 2.0 * mean_first * mean_second * mean_third
    )
    triple_cumulant = 1000.0 * kappa
    return (intra_rates, boundary[None, None], detector_load, triple_cumulant[None])


def solution(mesh):
    placed = (P("shot", "det"), P("det", None, None), P("det", None, None), P("det", None, None))
    shot_count = mesh.shape["shot"]
    det_count = mesh.shape["det"]
    power_of_two = shot_count & (shot_count - 1) == 0 and shot_count > 1
    whole_tiles = PB % shot_count == 0 and (PB // shot_count) % 8 == 0

    def body(events, pair_patches, pair_owners, triples):
        if power_of_two and whole_tiles and shot_count > 8 and triples.shape[1] % 128 == 0:
            return local_fused(events, pair_patches, pair_owners, triples, det_count)
        return local(events, pair_patches, pair_owners, triples)

    return jax.shard_map(
        body,
        mesh=mesh,
        in_specs=placed,
        out_specs=(
            P("det", "shot", None),
            P("det", "shot", None, None, None),
            P(None, "shot"),
            P("det", None),
        ),
        check_vma=False,
    )
```

```python
import functools

import jax
import jax.numpy as jnp
from jax import lax
from jax.experimental import pallas as pl
from jax.experimental.pallas import tpu as pltpu
from jax.sharding import PartitionSpec as P

PB = 128
VMEM_BYTES = 52 * 1024 * 1024


def fit_rates(coincide, row_count, col_count, shot_total):
    inverse = 1.0 / shot_total
    joint_rate = coincide * inverse
    row_rate = row_count[..., :, None] * inverse
    col_rate = col_count[..., None, :] * inverse
    denominator = jnp.maximum(1.0 - 2.0 * row_rate - 2.0 * col_rate + 4.0 * joint_rate, 0.25)
    excess = (joint_rate - row_rate * col_rate) / denominator
    return 100.0 * (0.5 - 0.5 * jnp.sqrt(jnp.maximum(1.0 - 4.0 * excess, 0.04)))


def route_table(owner_row, shot_count, recv_slots):
    owner_ids = jnp.arange(shot_count, dtype=jnp.int32)
    hit = owner_row[None, :] == owner_ids[:, None]
    entry_ids = jnp.arange(owner_row.shape[0], dtype=jnp.int32)
    upto = entry_ids[:, None] >= entry_ids[None, :]
    rank = jnp.sum(jnp.where(hit[:, None, :] & upto[None, :, :], 1, 0), axis=2) - 1
    slot_ids = jnp.arange(recv_slots, dtype=jnp.int32)
    chosen = hit[:, None, :] & (rank[:, None, :] == slot_ids[None, :, None])
    entry_pair = jnp.arange(owner_row.shape[0], dtype=jnp.int32) // 2
    pair_slot = jnp.sum(jnp.where(chosen, entry_pair[None, None, :], 0), axis=2)
    valid = jnp.any(chosen, axis=2).astype(jnp.float32)
    return (pair_slot, valid)


STREAMS = [
    ('pair', 0, (2, 1, 0), 7), ('pair', 0, (1, 0, 2), 5), ('pair', 0, (1, 0, 2), 7), ('pair', 0, (0, 2, 1), 7),
    ('pair', 1, (0, 1, 2), 5), ('pair', 1, (2, 0, 1), 13), ('pair', 1, (0, 2, 1), 8), ('intra', 0, (1, 2, 0, 3), 3),
    ('intra', 0, (1, 0, 2, 3), 5),
]
ORDER = [
    ('start', 4), ('start', 0), ('start', 1), ('start', 3), ('start', 2), ('start', 5), ('start', 6), ('triples', 0),
    (4, 0), (1, 0), (0, 0), ('triples', 1), ('start', 8), (3, 0), ('counts',), (2, 0), (4, 1), (6, 0), (0, 1), (5, 0),
    ('aux', 0), (1, 1), (3, 1), ('start', 7), (4, 2), (2, 1), (0, 2), ('aux', 1), (1, 2), (3, 2), (6, 1), (8, 0),
    (2, 2), (5, 1), (7, 0), ('aux', 2), (6, 2), (8, 1), (1, 3), (5, 2), (7, 1), (3, 3), ('aux', 3), (2, 3), (0, 3),
    ('route', 0), (8, 2), (4, 3), (7, 2), (6, 3), (5, 3), ('route', 1), (8, 3), (7, 3), ('intra',),
]


def plan_streams(patch_dev, pair_count):
    streams = [None] * len(STREAMS)
    for kind in (("pair", 0), ("pair", 1), ("intra", 0)):
        total = pair_count if kind[0] == "pair" else patch_dev
        members = [s for s, stream in enumerate(STREAMS) if stream[:2] == kind]
        whole = sum(STREAMS[s][3] for s in members)
        start, seen = 0, 0
        for s in members:
            seen += STREAMS[s][3]
            stop = total * seen // whole
            streams[s] = (*STREAMS[s][:3], start, stop - start)
            start = stop
    return streams


def finish_kernel(patch_dev, det_count, packed_in, intra_out, boundary_out, load_out, kappa_out,
                  load_buf, kappa_buf, out_sem):
    slots = boundary_out.shape[0]
    rows = intra_out.shape[0]
    parts = 3
    leave = []
    for i in range(parts):
        part = pl.ds(slots * i // parts, slots * (i + 1) // parts - slots * i // parts)
        leave.append(pltpu.make_async_copy(packed_in.at[part], boundary_out.at[part], out_sem.at[i]))
    leave.append(pltpu.make_async_copy(packed_in.at[slots, pl.ds(0, rows)], intra_out, out_sem.at[parts]))
    for copy in leave:
        copy.start()
    height = rows // patch_dev
    total = packed_in[slots, rows:rows + height]
    for d in range(1, det_count):
        total = total + packed_in[slots, rows + d * height:rows + (d + 1) * height]
    load_buf[...] = total[:, 0:load_out.shape[1]]
    first = rows + det_count * height
    for c in range(kappa_out.shape[1] // PB):
        kappa_buf[:, pl.ds(c * PB, PB)] = packed_in[slots, first + c:first + c + 1]
    small = [pltpu.make_async_copy(load_buf, load_out, out_sem.at[parts + 1]),
             pltpu.make_async_copy(kappa_buf, kappa_out, out_sem.at[parts + 2])]
    for copy in small:
        copy.start()
    for copy in leave + small:
        copy.wait()


def fused_kernel(plan, events_ref, tables_ref, packed_ref, *scratch):
    (streams, shot_count, det_count, patch_dev, pair_count, triple_count, recv_slots, load_chunks, tiles) = plan
    bits = shot_count.bit_length() - 1
    count = len(streams)
    raw, turned, aux, aux_in, intra_sum, pair_sum, turned_counts, row_buf, col_buf, fitted, outgoing, load_mine = scratch[:12]
    slot_vector, slot_table, ends_ref = scratch[12:15]
    (in_sem, send_sem, recv_sem, aux_send, aux_recv, out_send, out_recv, load_send, load_recv, relay,
     table_sem, ends_sem) = scratch[15:27]
    held = scratch[27:27 + count]
    landed = [scratch[27 + count + s * bits:27 + count + (s + 1) * bits] for s in range(count)]
    shot_dev, det_dev = raw.shape
    block_rows = PB // shot_count
    groups = shot_count // 2
    me = lax.axis_index("shot")
    my_det = lax.axis_index("det")
    shot_total = float(shot_dev * shot_count)
    inverse = 1.0 / shot_total
    bit = [(me // (1 << b)) % 2 for b in range(bits)]
    partner = [me + (1 - 2 * bit[b]) * (1 << b) for b in range(bits)]
    mesh_id = pl.DeviceIdType.MESH

    chunk = shot_dev // load_chunks
    copies = []
    for c in range(load_chunks):
        copy = pltpu.make_async_copy(
            events_ref.at[pl.ds(c * chunk, chunk), :], raw.at[pl.ds(c * chunk, chunk), :], in_sem.at[c])
        copy.start()
        copies.append(copy)
    ends_copy = pltpu.make_async_copy(tables_ref, ends_ref, ends_sem)
    ends_copy.start()
    barrier = pltpu.get_barrier_semaphore()
    for b in range(2):
        pl.semaphore_signal(barrier, inc=1, device_id={"shot": partner[b]}, device_id_type=mesh_id)
    has_up, has_down = me + 4 < shot_count, me >= 4

    def signal_line(sem):
        @pl.when(has_up)
        def _():
            pl.semaphore_signal(sem, inc=1, device_id={"shot": me + 4}, device_id_type=mesh_id)

        @pl.when(has_down)
        def _():
            pl.semaphore_signal(sem, inc=1, device_id={"shot": me - 4}, device_id_type=mesh_id)

    signal_line(barrier)
    line_count = has_up.astype(jnp.int32) + has_down.astype(jnp.int32)
    for d in range(1, det_count):
        pl.semaphore_signal(barrier, inc=1, device_id={"det": (my_det + d) % det_count}, device_id_type=mesh_id)

    def make_slot_table():
        lanes = 128
        lane = lax.broadcasted_iota(jnp.int32, (shot_count, lanes), 1)
        owner = lax.broadcasted_iota(jnp.int32, (shot_count, lanes), 0)
        hit_first = (tables_ref[2, :, 0:lanes] == owner).astype(jnp.int32)
        hit_second = (tables_ref[3, :, 0:lanes] == owner).astype(jnp.int32)
        both = hit_first + hit_second
        upto = both
        shift = 1
        while shift < pair_count:
            upto = upto + jnp.where(lane >= shift, pltpu.roll(upto, shift, 1), 0)
            shift *= 2
        rank_first = upto - both
        rank_second = rank_first + hit_first
        table = jnp.zeros((shot_count, lanes), jnp.int32)
        for j in range(recv_slots):
            pick = (jnp.where(rank_first == j, hit_first, 0) + jnp.where(rank_second == j, hit_second, 0))
            index = pair_count + jnp.sum(pick * (lane - pair_count), axis=1, keepdims=True)
            table = jnp.where(lane == j, index, table)
        slot_vector[...] = table
        copy = pltpu.make_async_copy(slot_vector, slot_table, table_sem)
        copy.start()
        return copy

    for c in range(load_chunks):
        copies[c].wait()
        piece = raw[pl.ds(c * chunk, chunk), :].astype(jnp.float32).T
        turned[:, :, pl.ds(c * chunk, chunk)] = piece.astype(jnp.bfloat16).reshape(patch_dev, PB, chunk)

    ends_copy.wait()
    nt = (((1,), (1,)), ((), ()))

    def stream_base(s, t):
        dims = streams[s][2]
        base = 0
        for i in range(t):
            base = base + bit[dims[i]] * (1 << (len(dims) - 1 - i))
        return base

    def stream_copy(s, t):
        dims = streams[s][2]
        if t == len(dims):
            source = held[s].at[pl.ds(stream_base(s, t), 1)]
            other = partner[bits - 1]
        else:
            length = 1 << (len(dims) - 1 - t)
            source = held[s].at[pl.ds(stream_base(s, t) + (1 - bit[dims[t]]) * length, length)]
            other = partner[dims[t]]
        return pltpu.make_async_remote_copy(
            src_ref=source, dst_ref=landed[s][t], send_sem=send_sem.at[s, t], recv_sem=recv_sem.at[s, t],
            device_id={"shot": other}, device_id_type=mesh_id)

    def place(dims, g):
        return sum(((g >> dims[i]) & 1) << (len(dims) - 1 - i) for i in range(len(dims)))

    owner_of = {}
    for s, (kind, tile, _, start, size) in enumerate(streams):
        for k in range(size):
            owner_of[kind, tile, start + k] = (s, k)
    done = set()

    def put(s):
        kind, _, _, start, size = streams[s]
        for k in range(start, start + size):
            if (kind, k) in done:
                continue
            done.add((kind, k))
            if kind == "intra":
                left, right = turned[k], turned[k]
            else:
                left, right = turned[ends_ref[0, 0, k]], turned[ends_ref[1, 0, k]]
            gram = lax.dot_general(left, right, nt, preferred_element_type=jnp.float32)
            if kind == "intra":
                where = [(0, g, g) for g in range(shot_count)]
            else:
                where = [(i, g, i * groups + g) for i in range(tiles) for g in range(groups)]
            for i, g, row in where:
                to, at = owner_of[kind, i, k]
                held[to][place(streams[to][2], g), at] = gram[row * block_rows:(row + 1) * block_rows]

    lead = []
    for op in ORDER:
        if op[0] != "start":
            break
        lead.append(op[1])
    waits = ["relay"]

    def send(s, t):
        dims = streams[s][2]
        if waits and (t == len(dims) or dims[t] == bits - 1):
            waits.clear()
            pl.semaphore_wait(relay, line_count)
        stream_copy(s, t).start()

    for n, s in enumerate(lead):
        put(s)
        if n == 0:
            pl.semaphore_wait(barrier, 2 + line_count + det_count - 1)
            signal_line(relay)
        send(s, 0)
    for s in range(count):
        put(s)

    def triple_counts(c):
        column = lax.broadcasted_iota(jnp.int32, (128, det_dev), 1)
        lane = lax.broadcasted_iota(jnp.int32, (128, 128), 1)
        bit_rows = []
        for m in range(3):
            named = jnp.broadcast_to(tables_ref[4 + m, :, pl.ds(c * 128, 128)], (128, 128)).T[:, 0:1]
            bit_rows.append(
                jnp.dot((named == column).astype(jnp.float32).astype(jnp.bfloat16),
                        turned[...].reshape(det_dev, shot_dev), preferred_element_type=jnp.float32))
        one, two, three = bit_rows
        both = one * two
        terms = [one, two, three, both, one * three, two * three, both * three]
        packed = jnp.zeros((128, 128), jnp.float32)
        for q, term in enumerate(terms):
            packed = jnp.where(lane == q, jnp.sum(term, axis=1, keepdims=True), packed)
        aux[0, pl.ds(patch_dev + 8 * c, 8), :] = packed.T[0:8]

    def aux_copy(t):
        return pltpu.make_async_remote_copy(
            src_ref=aux.at[t], dst_ref=aux_in.at[t], send_sem=aux_send.at[t], recv_sem=aux_recv.at[t],
            device_id={"shot": partner[t]}, device_id_type=mesh_id)

    pending = []

    def send_aux():
        ones = jnp.ones((8, shot_dev), jnp.bfloat16)
        for p in range(patch_dev):
            total = lax.dot_general(ones, turned[p], nt, preferred_element_type=jnp.float32)
            aux[0, pl.ds(p, 1), :] = total[0:1]
        aux_copy(0).start()
        pending.append(make_slot_table())

    unfitted = []
    means = []

    def fit_pairs():
        while means and unfitted:
            _, i, _, start, size = streams[unfitted.pop()]
            for k in range(start, start + size):
                fitted[i, k] = rates(pair_sum[i, k], row_buf[i, ends_ref[0, 0, k]], col_buf[ends_ref[1, 0, k]])

    def step(s, t):
        kind, tile, dims, start, size = streams[s]
        depth = len(dims)
        stream_copy(s, t).wait_recv()
        base = stream_base(s, min(t + 1, depth))
        if t == depth:
            pair_sum[tile, pl.ds(start, size)] = held[s][base] + landed[s][t][0]
            unfitted.append(s)
            fit_pairs()
        elif t == depth - 1 and kind == "intra":
            intra_sum[pl.ds(start, size)] = held[s][base] + landed[s][t][0]
        elif t == depth - 1:
            held[s][base] = held[s][base] + landed[s][t][0]
            send(s, t + 1)
        else:
            half = 1 << (depth - 2 - t)
            away = (1 - bit[dims[t + 1]]) * half
            keep = bit[dims[t + 1]] * half

            def add(part):
                mine = pl.ds(base + part, half)
                held[s][mine] = held[s][mine] + landed[s][t][pl.ds(part, half)]
            add(away)
            send(s, t + 1)
            add(keep)

    def rates(coincide, row_rate, col_rate):
        joint_rate = coincide * inverse
        denominator = jnp.maximum(1.0 - 2.0 * row_rate - 2.0 * col_rate + 4.0 * joint_rate, 0.25)
        excess = (joint_rate - row_rate * col_rate) / denominator
        return 100.0 * (0.5 - 0.5 * jnp.sqrt(jnp.maximum(1.0 - 4.0 * excess, 0.04)))

    my_group = me % groups

    def tile_row(i):
        return pl.multiple_of((i * groups + my_group) * block_rows, block_rows)

    def make_means():
        rows = aux[bits]
        turned_counts[...] = jnp.concatenate(
            [rows * inverse, jnp.zeros((PB - rows.shape[0], PB), jnp.float32)], axis=0).T
        starts = [tile_row(i) for i in range(tiles)] + [pl.multiple_of(me * block_rows, block_rows)]
        for i, row in enumerate(starts):
            piece = turned_counts[pl.ds(row, block_rows), :]
            for p in range(patch_dev):
                row_buf[i, p] = jnp.broadcast_to(piece[:, p:p + 1], (block_rows, PB))
        for p in range(patch_dev):
            col_buf[p] = jnp.broadcast_to(aux[bits, pl.ds(p, 1), :] * inverse, (block_rows, PB))
        fitted[:, pair_count] = jnp.zeros((tiles, block_rows, PB), jnp.float32)
        for c in range(triple_count // 128):
            sums = aux[bits, pl.ds(patch_dev + 8 * c, 8), :] * inverse
            first, second, third = sums[0:1], sums[1:2], sums[2:3]
            kappa = (sums[6:7] - sums[3:4] * third - sums[4:5] * second - sums[5:6] * first
                     + 2.0 * first * second * third)
            row = (patch_dev + det_count) * block_rows + c
            packed_ref[recv_slots, row:row + 1, :] = 1000.0 * kappa

    def out_copy(i, m):
        other = me
        for b in range(bits - 1):
            if (m >> b) & 1:
                other = other + (1 - 2 * bit[b]) * (1 << b)
        return other, pltpu.make_async_remote_copy(
            src_ref=outgoing.at[i, m], dst_ref=packed_ref.at[pl.ds(0, recv_slots), pl.ds(tile_row(i), block_rows), :],
            send_sem=out_send.at[i, m], recv_sem=out_recv.at[i, m],
            device_id={"shot": other}, device_id_type=mesh_id)

    def route(i):
        if pending:
            pending.pop().wait()

        for m in reversed(range(1, groups)):
            other, copy = out_copy(i, m)
            for j in range(recv_slots):
                outgoing[i, m, j] = fitted[i, slot_table[other, j]]
            copy.start()
        for j in range(recv_slots):
            packed_ref[j, pl.ds(tile_row(i), block_rows), :] = fitted[i, slot_table[me, j]]

    load_rows = pl.ds(pl.multiple_of((patch_dev + my_det) * block_rows, block_rows), block_rows)

    def load_copy(d):
        return pltpu.make_async_remote_copy(
            src_ref=load_mine, dst_ref=packed_ref.at[recv_slots, load_rows, :], send_sem=load_send.at[d], recv_sem=load_recv.at[d],
            device_id={"det": (my_det + d) % det_count}, device_id_type=mesh_id)

    def finish_intra():
        col = lax.broadcasted_iota(jnp.int32, (block_rows, PB), 1)
        loads = jnp.zeros((block_rows, PB), jnp.float32)
        for p in range(patch_dev):
            fit = rates(intra_sum[p], row_buf[tiles, p], col_buf[p])
            packed_ref[recv_slots, p * block_rows:(p + 1) * block_rows, :] = fit
            loads = jnp.where(col == my_det * patch_dev + p, jnp.sum(fit, axis=1, keepdims=True), loads)
        load_mine[...] = loads
        for d in range(1, det_count):
            load_copy(d).start()
        packed_ref[recv_slots, load_rows, :] = loads

    for op in ORDER[len(lead):]:
        if op[0] == "start":
            send(op[1], 0)
        elif op[0] == "triples":
            for c in range(op[1], triple_count // 128, 2):
                triple_counts(c)
        elif op[0] == "counts":
            send_aux()
        elif op[0] == "aux":
            t = op[1]
            aux_copy(t).wait_recv()
            aux[t + 1] = aux[t] + aux_in[t]
            if t == bits - 1:
                make_means()
                means.append(True)
                fit_pairs()
            else:
                if t == bits - 2 and waits:
                    waits.clear()
                    pl.semaphore_wait(relay, line_count)
                aux_copy(t + 1).start()
        elif op[0] == "route":
            route(op[1])
        elif op[0] == "intra":
            finish_intra()
        else:
            step(*op)

    for t in range(bits):
        aux_copy(t).wait_send()
        for s in range(count):
            stream_copy(s, t).wait_send()
    for d in range(1, det_count):
        load_copy(d).wait()
    for i in range(tiles):
        for m in range(1, groups):
            out_copy(i, m)[1].wait()


def local_fused(events, pair_patches, pair_owners, triples, det_count):
    shot_dev, det_dev = events.shape
    shot_count = lax.axis_size("shot")
    bits = shot_count.bit_length() - 1
    patch_dev = det_dev // PB
    block_rows = PB // shot_count
    pair_count = pair_patches.shape[1]
    triple_count = triples.shape[1]
    recv_slots = max(2, 4 * pair_count // shot_count)
    streams = plan_streams(patch_dev, pair_count)
    load_chunks = 4
    tiles = 2
    vmem = pl.BlockSpec(memory_space=pltpu.VMEM)
    plan = (streams, shot_count, det_count, patch_dev, pair_count, triple_count, recv_slots, load_chunks, tiles)
    aux_rows = patch_dev + 8 * (triple_count // 128)
    f32 = jnp.float32
    dma = pltpu.SemaphoreType.DMA
    count = len(streams)
    tile = (block_rows, PB)
    scratch = [
        pltpu.VMEM((shot_dev, det_dev), jnp.int32),
        pltpu.VMEM((patch_dev, PB, shot_dev), jnp.bfloat16),
        pltpu.VMEM((bits + 1, aux_rows, 128), f32),
        pltpu.VMEM((bits, aux_rows, 128), f32),
        pltpu.VMEM((patch_dev, *tile), f32),
        pltpu.VMEM((tiles, pair_count, *tile), f32),
        pltpu.VMEM((PB, PB), f32),
        pltpu.VMEM((tiles + 1, patch_dev, *tile), f32),
        pltpu.VMEM((patch_dev, *tile), f32),
        pltpu.VMEM((tiles, pair_count + 1, *tile), f32),
        pltpu.VMEM((tiles, shot_count // 2, recv_slots, *tile), f32),
        pltpu.VMEM(tile, f32),
        pltpu.VMEM((shot_count, 128), jnp.int32),
        pltpu.SMEM((shot_count, 128), jnp.int32),
        pltpu.SMEM((7, 1, triple_count), jnp.int32),
        dma((load_chunks,)), dma((count, bits)), dma((count, bits)), dma((bits,)), dma((bits,)),
        dma((tiles, shot_count // 2)), dma((tiles, shot_count // 2)), dma((det_count,)), dma((det_count,)),
        pltpu.SemaphoreType.REGULAR, dma, dma,
    ]
    scratch += [pltpu.VMEM((1 << len(dims), size, *tile), f32) for _, _, dims, _, size in streams]
    for _, _, dims, _, size in streams:
        scratch += [pltpu.VMEM((max(1, (1 << len(dims)) >> (t + 1)), size, *tile), f32) for t in range(bits)]
    def lanes(rows, fill):
        rows = jnp.transpose(rows, (2, 0, 1))
        return jnp.pad(rows, ((0, 0), (0, 0), (0, triple_count - pair_count)), constant_values=fill)

    tables = jnp.concatenate(
        [lanes(pair_patches, 0), lanes(pair_owners, -1), jnp.transpose(triples, (2, 0, 1))], axis=0)
    packed = pl.pallas_call(
        functools.partial(fused_kernel, plan),
        out_shape=jax.ShapeDtypeStruct((recv_slots + 1, PB, PB), f32),
        in_specs=[pl.BlockSpec(memory_space=pltpu.HBM), vmem],
        out_specs=vmem,
        scratch_shapes=scratch,
        compiler_params=pltpu.CompilerParams(
            collective_id=0, has_side_effects=True, vmem_limit_bytes=VMEM_BYTES),
    )(events, tables)
    hbm = pl.BlockSpec(memory_space=pltpu.HBM)
    intra, boundary, load, kappa = pl.pallas_call(
        functools.partial(finish_kernel, patch_dev, det_count),
        out_shape=(
            jax.ShapeDtypeStruct((patch_dev * block_rows, PB), f32),
            jax.ShapeDtypeStruct((recv_slots, PB, PB), f32),
            jax.ShapeDtypeStruct((block_rows, det_count * patch_dev), f32),
            jax.ShapeDtypeStruct((1, triple_count), f32),
        ),
        in_specs=[vmem],
        out_specs=(hbm, hbm, hbm, hbm),
        scratch_shapes=[
            pltpu.VMEM((block_rows, det_count * patch_dev), f32), pltpu.VMEM((1, triple_count), f32), dma((6,))],
        compiler_params=pltpu.CompilerParams(vmem_limit_bytes=4 * 1024 * 1024),
    )(packed)
    return (intra.reshape(patch_dev, block_rows, PB), boundary[None, None], jnp.swapaxes(load, 0, 1), kappa)


def local(events, pair_patches, pair_owners, triples):
    shot_dev, det_dev = events.shape
    shot_count = lax.axis_size("shot")
    shot_index = lax.axis_index("shot")
    shot_total = float(shot_dev * shot_count)
    inverse = 1.0 / shot_total
    patch_dev = det_dev // PB
    rows_own = PB // shot_count
    pair_count = pair_patches.shape[1]
    triple_count = triples.shape[1]
    recv_slots = max(2, 4 * pair_count // shot_count)
    bit_matrix = events.astype(jnp.bfloat16)
    patches = bit_matrix.reshape(shot_dev, patch_dev, PB)
    local_counts = jnp.sum(events, axis=0).astype(jnp.float32)
    triple_index = triples[0]
    picked = (
        jnp.take(events, triple_index.reshape(-1), axis=1)
        .astype(jnp.float32)
        .reshape(shot_dev, triple_count, 3)
    )
    first_bit = picked[:, :, 0]
    second_bit = picked[:, :, 1]
    third_bit = picked[:, :, 2]
    triple_terms = jnp.stack(
        [
            jnp.sum(first_bit * second_bit, axis=0),
            jnp.sum(first_bit * third_bit, axis=0),
            jnp.sum(second_bit * third_bit, axis=0),
            jnp.sum(first_bit * second_bit * third_bit, axis=0),
        ]
    )
    intra = jnp.einsum("sai,saj->aij", patches, patches, preferred_element_type=jnp.float32)
    pair_ends = pair_patches[0]

    def pair_gram(ends):
        first = lax.dynamic_slice_in_dim(bit_matrix, ends[0] * PB, PB, 1)
        second = lax.dynamic_slice_in_dim(bit_matrix, ends[1] * PB, PB, 1)
        return lax.dot_general(first, second, (((0,), (0,)), ((), ())), preferred_element_type=jnp.float32)

    cross = lax.map(pair_gram, pair_ends)
    joined = lax.psum_scatter(
        jnp.concatenate([intra, cross], axis=0), "shot", scatter_dimension=1, tiled=True
    )
    intra_share = joined[:patch_dev]
    pair_share = joined[patch_dev:]
    counts, triple_total = lax.psum((local_counts, triple_terms), "shot")
    patch_counts = counts.reshape(patch_dev, PB)
    row_counts = lax.dynamic_slice_in_dim(patch_counts, shot_index * rows_own, rows_own, 1)
    intra_rates = fit_rates(intra_share, row_counts, patch_counts, shot_total)
    load_share = jnp.sum(intra_rates, axis=2)
    detector_load = lax.all_gather(load_share, "det", axis=0, tiled=True)
    pair_slot, valid = route_table(pair_owners[0].reshape(-1), shot_count, recv_slots)
    mine = lax.dynamic_index_in_dim(pair_slot, shot_index, 0, keepdims=False)
    valid_mine = lax.dynamic_index_in_dim(valid, shot_index, 0, keepdims=False)
    fitted = fit_rates(
        pair_share,
        jnp.take(row_counts, pair_ends[:, 0], axis=0),
        jnp.take(patch_counts, pair_ends[:, 1], axis=0),
        shot_total,
    )
    every_block = lax.all_gather(fitted, "shot", axis=1, tiled=True)
    boundary = lax.map(lambda k: lax.dynamic_index_in_dim(every_block, k, 0, keepdims=False), mine)
    boundary = boundary * valid_mine[:, None, None]
    moments = triple_total * inverse
    means = jnp.take(counts, triple_index.reshape(-1), axis=0).reshape(triple_count, 3) * inverse
    mean_first = means[:, 0]
    mean_second = means[:, 1]
    mean_third = means[:, 2]
    kappa = (
        moments[3]
        - moments[0] * mean_third
        - moments[1] * mean_second
        - moments[2] * mean_first
        + 2.0 * mean_first * mean_second * mean_third
    )
    triple_cumulant = 1000.0 * kappa
    return (intra_rates, boundary[None, None], detector_load, triple_cumulant[None])


def solution(mesh):
    placed = (P("shot", "det"), P("det", None, None), P("det", None, None), P("det", None, None))
    shot_count = mesh.shape["shot"]
    det_count = mesh.shape["det"]
    power_of_two = shot_count & (shot_count - 1) == 0 and shot_count > 1
    whole_tiles = PB % shot_count == 0 and (PB // shot_count) % 8 == 0

    def body(events, pair_patches, pair_owners, triples):
        if power_of_two and whole_tiles and shot_count > 8 and triples.shape[1] % 128 == 0:
            return local_fused(events, pair_patches, pair_owners, triples, det_count)
        return local(events, pair_patches, pair_owners, triples)

    return jax.shard_map(
        body,
        mesh=mesh,
        in_specs=placed,
        out_specs=(
            P("det", "shot", None),
            P("det", "shot", None, None, None),
            P(None, "shot"),
            P("det", None),
        ),
        check_vma=False,
    )
```
